32 devices in a mesh: expert: 8 (over z, x), hidden: 4 (over y, core).
Axes of the slice: x: 2, y: 2, z: 4, core: 2. Of those that a mesh axis runs over, the one named last changes fastest.
Arguments:
- tokens: bfloat16 [32, 196, 1024], P(('expert', 'hidden')), may hold values from -40 to 40
- router: bfloat16 [1024, 8], replicated, may hold values from -0.5 to 0.5
- w_in: bfloat16 [8, 1024, 3072], P('expert', None, 'hidden'), may hold values from -0.1875 to 0.1875
- b_in: float32 [8, 3072], P('expert', 'hidden'), may hold values from -6 to 6
- w_out: bfloat16 [8, 3072, 1024], P('expert', 'hidden'), may hold values from -0.109375 to 0.109375
- cotangent: bfloat16 [32, 196, 1024], P(('expert', 'hidden')), may hold values from -6 to 6
Outputs:
- mixed: bfloat16 [32, 196, 1024], P(('expert', 'hidden'))
- token_grad: bfloat16 [32, 196, 1024], P(('expert', 'hidden'))
The draws below stay inside these ranges and needn't reach their ends.
All inputs are finite; a program needn't handle non-finite values.
Results may differ from the reference program's by a relative error of at most 0.015.
Values may be sent and summed in bfloat16 or wider, within the bound.
A program may use at most 64 MiB of HBM per device.

```python
import math
import jax
import jax.numpy as jnp
from jax import lax

D = 1024
FF = 3072
M = 196
EXPERTS = 8
IMAGES = 32
N_HIDDEN = 4


def build_router(key):
    inner = jax.random.fold_in(key, 11)
    raw = jax.random.normal(inner, (D, EXPERTS), jnp.float32) * (2.0 / math.sqrt(D))
    return jnp.clip(raw, -0.5, 0.5).astype(jnp.bfloat16).astype(jnp.float32)


def draw_router(key, part):
    return build_router(key).astype(jnp.bfloat16)


def draw_tokens(key, part):
    inner = jax.random.fold_in(key, 23)
    base = jnp.clip(jax.random.normal(inner, (IMAGES, M, D), jnp.float32), -6.0, 6.0)
    return jnp.clip(base, -40.0, 40.0).astype(jnp.bfloat16)


def block_levels(key, dims, cuts, least, largest):
    level = 1.0
    for dim, blocks in cuts:
        heights = jax.random.uniform(jax.random.fold_in(jax.random.fold_in(key, 6), dim), (blocks,), jnp.float32, least / len(cuts), largest / len(cuts))
        level = level * jnp.repeat(jnp.exp(heights), dims[dim] // blocks).reshape((-1,) + (1,) * (len(dims) - 1 - dim))
    return level


def scatter_about(rng, extent, width, most, cuts=(), held_as=jnp.bfloat16):
    values = width * jax.random.normal(rng, extent, jnp.float32)
    if cuts:
        values = values * block_levels(rng, extent, cuts, -0.22, 0.18)
    return jnp.clip(values, -most, most).astype(held_as)


def setup_inputs(seed: int = 0) -> dict:
    arg_keys = jax.random.split(jax.random.key(seed), 7)
    return {
        "tokens": draw_tokens(jax.random.fold_in(arg_keys[6], 71), 0),
        "router": draw_router(jax.random.fold_in(arg_keys[6], 71), 0),
        "w_in": scatter_about(arg_keys[2], (EXPERTS, D, FF), D ** -0.5, 0.1875, ((0, 8), (2, 4))),
        "b_in": scatter_about(arg_keys[3], (EXPERTS, FF), 1.0, 6.0, ((0, 8), (1, 4)), jnp.float32),
        "w_out": scatter_about(arg_keys[4], (EXPERTS, FF, D), FF ** -0.5, 0.109375, ((0, 8), (1, 4))),
        "cotangent": scatter_about(arg_keys[5], (IMAGES, M, D), 1.0, 6.0, ((0, 32),)),
    }


def expert_rows(packed):
    rows, grads, weight_in, bias_in, weight_out = packed
    count = rows.shape[0]
    quarter = FF // N_HIDDEN
    pre = jnp.dot(rows, weight_in, preferred_element_type=jnp.float32) + bias_in
    act = jax.nn.gelu(pre).astype(jnp.bfloat16)
    parts = jnp.einsum('bhf,hfd->hbd', act.reshape(count, N_HIDDEN, quarter).astype(jnp.float32), weight_out.reshape(N_HIDDEN, quarter, D).astype(jnp.float32)).astype(jnp.bfloat16)
    slot_out = lax.optimization_barrier(jnp.sum(parts.astype(jnp.float32), axis=0)).astype(jnp.bfloat16)
    act_grad = jnp.dot(grads, weight_out.T, preferred_element_type=jnp.float32)
    _, pull = jax.vjp(jax.nn.gelu, pre)
    pre_grad = pull(act_grad)[0].astype(jnp.bfloat16)
    gparts = jnp.einsum('bhf,dhf->hbd', pre_grad.reshape(count, N_HIDDEN, quarter).astype(jnp.float32), weight_in.reshape(D, N_HIDDEN, quarter).astype(jnp.float32)).astype(jnp.bfloat16)
    slot_grad = lax.optimization_barrier(jnp.sum(gparts.astype(jnp.float32), axis=0)).astype(jnp.bfloat16)
    return (slot_out, slot_grad)

def reference(tokens, router, w_in, b_in, w_out, cotangent):
    tok32 = tokens.astype(jnp.float32)
    cot32 = cotangent.astype(jnp.float32)
    router32 = router.astype(jnp.float32)
    logits = jnp.einsum('bmd,ds->bms', tok32, router32)
    dispatch = jax.nn.softmax(logits, axis=1)
    combine = jax.nn.softmax(logits, axis=2)
    dispatch_w = dispatch.astype(jnp.bfloat16)
    combine_w = combine.astype(jnp.bfloat16)
    slot_in = jnp.einsum('bms,bmd->bsd', dispatch_w.astype(jnp.float32), tok32).astype(jnp.bfloat16)
    slot_cot = jnp.einsum('bms,bmd->bsd', combine_w.astype(jnp.float32), cot32).astype(jnp.bfloat16)
    slot_out, slot_grad = lax.map(expert_rows, (jnp.transpose(slot_in, (1, 0, 2)), jnp.transpose(slot_cot, (1, 0, 2)), w_in, b_in, w_out))
    slot_out = jnp.transpose(slot_out, (1, 0, 2)).astype(jnp.float32)
    slot_grad = jnp.transpose(slot_grad, (1, 0, 2)).astype(jnp.float32)
    mixed = jnp.einsum('bms,bsd->bmd', combine_w.astype(jnp.float32), slot_out).astype(jnp.bfloat16)
    combine_grad = jnp.einsum('bmd,bsd->bms', cot32, slot_out)
    dispatch_grad = jnp.einsum('bmd,bsd->bms', tok32, slot_grad)
    logit_grad = combine * (combine_grad - lax.optimization_barrier(jnp.sum(combine * combine_grad, axis=2, keepdims=True)))
    logit_grad = logit_grad + dispatch * (dispatch_grad - lax.optimization_barrier(jnp.sum(dispatch * dispatch_grad, axis=1, keepdims=True)))
    logit_grad = logit_grad.astype(jnp.bfloat16)
    token_grad = jnp.einsum('bms,bsd->bmd', dispatch_w.astype(jnp.float32), slot_grad)
    token_grad = token_grad + jnp.einsum('bms,ds->bmd', logit_grad.astype(jnp.float32), router32)
    return (mixed, token_grad.astype(jnp.bfloat16))
```

```python
import functools
import math

import jax
import jax.numpy as jnp
from jax import lax
from jax.experimental import pallas as pl
from jax.experimental.pallas import tpu as pltpu
from jax.sharding import PartitionSpec as P

MESH = pl.DeviceIdType.MESH
BF = jnp.bfloat16
F32 = jnp.float32
LANES = 128
VMEM_BYTES = 67043328
SLACK = 4096


def dot(a, b, ca, cb):
    return lax.dot_general(a, b, (((ca,), (cb,)), ((), ())), preferred_element_type=F32)


def scatter_rows(scr, base, value, period):
    rows, width = value.shape
    for c in range(width // LANES):
        scr[pl.ds(base + c, rows, stride=period), :] = value[:, c * LANES : (c + 1) * LANES]


def gather_rows(scr, base, rows, chunks, period):
    parts = [scr[pl.ds(base + c, rows, stride=period), :] for c in range(chunks)]
    return jnp.concatenate(parts, axis=1)


def each_peer(n_exp, n_hid, my_e, my_h, act):
    def flip(mine, by, size):
        bit, out = 1, mine
        while bit < size:
            out = out + lax.rem(by // bit, 2) * (bit - 2 * bit * lax.rem(mine // bit, 2))
            bit *= 2
        return out

    hids = [flip(my_h, jnp.int32(j), n_hid) for j in range(n_hid)]

    def step(k, carry):
        e = flip(my_e, n_exp - k, n_exp)
        for j in reversed(range(n_hid)):
            act(e, hids[j])
        return carry

    lax.fori_loop(1, n_exp, step, 0, unroll=n_exp <= 8)
    for j in reversed(range(1, n_hid)):
        act(my_e, hids[j])


def batch_cuts(n_exp):
    return (0, 1, n_exp)


def kernel(
    n_exp, n_hid,
    tok_hbm, rt_hbm, wi_hbm, bi_hbm, wo_hbm, cot_hbm,
    tok_t, cot_t, rt, dispatch_ref, combine_ref, combine_t, slot_out, slot_grad,
    tok, cot, wi, bi, wo, wi_t, wo_t, scr_a, send_buf, recv, scr_b, out_buf, ret,
    load_sem, send_sem, recv_sem,
):
    n = n_exp * n_hid
    my_e, my_h = lax.axis_index("expert"), lax.axis_index("hidden")
    me = my_e * n_hid + my_h
    width = tok.shape[1]
    chunks = width // LANES
    period = 2 * chunks

    loads = [
        pltpu.make_async_copy(tok_hbm.at[0], tok, load_sem.at[0]),
        pltpu.make_async_copy(rt_hbm, rt, load_sem.at[1]),
        pltpu.make_async_copy(cot_hbm.at[0], cot, load_sem.at[2]),
        pltpu.make_async_copy(wi_hbm.at[0], wi, load_sem.at[3]),
        pltpu.make_async_copy(bi_hbm, bi, load_sem.at[4]),
        pltpu.make_async_copy(wo_hbm.at[0], wo, load_sem.at[5]),
    ]
    for load in loads[:3]:
        load.start()

    barrier = pltpu.get_barrier_semaphore()

    def greet(k, _):
        dest = lax.rem(me + k, n)
        pl.semaphore_signal(
            barrier, inc=1, device_id=(dest // n_hid, lax.rem(dest, n_hid)), device_id_type=MESH
        )
        return 0

    lax.fori_loop(1, n, greet, 0, unroll=n <= 32)
    for load in loads[3:]:
        load.start()

    loads[0].wait()
    loads[1].wait()
    rt_t = rt[...]
    logits = dot(rt_t, tok[...], 1, 1)
    up = jnp.exp(logits - jnp.max(logits, axis=1, keepdims=True))
    dispatch = up / jnp.sum(up, axis=1, keepdims=True)
    up = jnp.exp(logits - jnp.max(logits, axis=0, keepdims=True))
    combine = up / jnp.sum(up, axis=0, keepdims=True)
    dispatch_ref[...] = dispatch
    combine_ref[...] = combine
    dispatch_w = dispatch.astype(BF)
    combine_w = combine.astype(BF)

    scatter_rows(scr_a, 0, dot(dispatch_w, tok[...], 1, 0), period)
    loads[2].wait()
    scatter_rows(scr_a, chunks, dot(combine_w, cot[...], 1, 0), period)
    send_buf[...] = scr_a[...].reshape(send_buf.shape).astype(BF)

    cuts = batch_cuts(n_exp)
    my_batch = sum((my_e >= low).astype(jnp.int32) for low in cuts[1:-1])
    pl.semaphore_wait(barrier, n - 1)

    def send_slots(e, h):
        pltpu.make_async_remote_copy(
            src_ref=send_buf.at[e],
            dst_ref=recv.at[me],
            send_sem=send_sem.at[0],
            recv_sem=recv_sem.at[my_batch],
            device_id=(e, h),
            device_id_type=MESH,
        ).start()

    each_peer(n_exp, n_hid, my_e, my_h, send_slots)
    pltpu.make_async_copy(send_buf.at[my_e], recv.at[me], recv_sem.at[my_batch]).start()

    combine_t[...] = combine.T.astype(BF)
    for i in (3, 4, 5):
        loads[i].wait()
    wi_t[...] = wi[...].T
    wo_t[...] = wo[...].T
    tok_t[...] = tok[...].T
    cot_t[...] = cot[...].T

    scale, cubic = math.sqrt(2.0 / math.pi), 0.044715
    others = pl.ds(0, n - 1)
    back_sem = len(cuts) - 1
    for b, (low, high) in enumerate(zip(cuts, cuts[1:])):
        first, rows = low * n_hid, (high - low) * n_hid
        span = pl.ds(first, rows)
        pltpu.make_async_copy(recv.at[span], recv.at[span], recv_sem.at[b]).wait()

        base = first * period
        scr_b[pl.ds(base, rows * period), :] = recv[span].astype(F32).reshape(rows * period, LANES)
        rows_in = gather_rows(scr_b, base, rows, chunks, period).astype(BF)
        rows_cot = gather_rows(scr_b, base + chunks, rows, chunks, period).astype(BF)
        pre = dot(rows_in, wi[...], 1, 0) + bi[...]
        act_grad = dot(rows_cot, wo_t[...], 1, 0)
        square = pre * pre
        tanh = jnp.tanh(scale * (pre + cubic * (square * pre)))
        cdf = 0.5 * (1.0 + tanh)
        act = (pre * cdf).astype(BF)
        slope = cdf + 0.5 * pre * (1.0 - tanh * tanh) * (scale * (1.0 + (3.0 * cubic) * square))
        pre_grad = (act_grad * slope).astype(BF)
        scatter_rows(scr_b, base, dot(act, wo[...], 1, 0), period)
        scatter_rows(scr_b, base + chunks, dot(pre_grad, wi_t[...], 1, 0), period)
        out_buf[span] = scr_b[pl.ds(base, rows * period), :].reshape((rows,) + out_buf.shape[1:]).astype(BF)

        def send_back(e, h):
            @pl.when(jnp.logical_and(e >= low, e < high))
            def _():
                pltpu.make_async_remote_copy(
                    src_ref=out_buf.at[e * n_hid + h],
                    dst_ref=ret.at[me],
                    send_sem=send_sem.at[1],
                    recv_sem=recv_sem.at[back_sem],
                    device_id=(e, h),
                    device_id_type=MESH,
                ).start()

        each_peer(n_exp, n_hid, my_e, my_h, send_back)
    ret[me] = out_buf[me]
    pltpu.make_async_copy(ret.at[others], ret.at[others], recv_sem.at[back_sem]).wait()

    total = jnp.sum(ret[...].astype(F32).reshape((n_exp, n_hid) + ret.shape[1:]), axis=1)
    scr_a[...] = total.reshape(scr_a.shape)
    slot_out[...] = gather_rows(scr_a, 0, n_exp, chunks, period).astype(BF)
    slot_grad[...] = gather_rows(scr_a, chunks, n_exp, chunks, period).astype(BF)

    sent = send_buf if n - 1 <= n_exp else out_buf
    for i in range(2):
        pltpu.make_async_copy(sent.at[others], sent.at[others], send_sem.at[i]).wait()


def finish(tok_t, cot_t, rt, dispatch_ref, combine_ref, combine_t, slot_out, slot_grad,
           mixed_hbm, grad_hbm, mixed_v, grad_v, out_sem):
    dispatch, combine = dispatch_ref[...], combine_ref[...]
    mixed_v[...] = dot(combine_t[...], slot_out[...], 1, 0).astype(BF)
    put_mixed = pltpu.make_async_copy(mixed_v, mixed_hbm.at[0], out_sem.at[0])
    put_mixed.start()
    combine_grad = dot(slot_out[...], cot_t[...], 1, 0)
    dispatch_grad = dot(slot_grad[...], tok_t[...], 1, 0)
    logit_grad = combine * (combine_grad - jnp.sum(combine * combine_grad, axis=0, keepdims=True))
    logit_grad = logit_grad + dispatch * (
        dispatch_grad - jnp.sum(dispatch * dispatch_grad, axis=1, keepdims=True)
    )
    left = jnp.concatenate([dispatch, logit_grad], axis=0).T.astype(BF)
    right = jnp.concatenate([slot_grad[...], rt[...]], axis=0)
    tokens = left.shape[0]
    half = -(-tokens // 32) * 16
    puts = [put_mixed]
    for i, (low, size) in enumerate(((0, half), (half, tokens - half))):
        span = pl.ds(low, size)
        grad_v[span, :] = dot(left[low : low + size], right, 1, 0).astype(BF)
        put = pltpu.make_async_copy(grad_v.at[span], grad_hbm.at[0, span], out_sem.at[1 + i])
        put.start()
        puts.append(put)
    for put in puts:
        put.wait()


def shards(n_exp, n_hid, tokens, router, w_in, b_in, w_out, cotangent):
    n = n_exp * n_hid
    _, m, d = tokens.shape
    f = w_in.shape[2]
    period = 2 * d // LANES
    assert tokens.shape[0] == 1 and w_in.shape[0] == 1
    any_spec = pl.BlockSpec(memory_space=pl.ANY)
    vmem_spec = pl.BlockSpec(memory_space=pltpu.VMEM)
    kept = [((d, m), BF)] * 2 + [((n_exp, d), BF)] + [((n_exp, m), F32)] * 2 + [((m, n_exp), BF)] + [((n_exp, d), BF)] * 2
    held = sum(-(-r // 8) * 8 * -(-c // LANES) * LANES * jnp.dtype(t).itemsize for (r, c), t in kept)
    grant = VMEM_BYTES - held - SLACK
    handed = pl.pallas_call(
        functools.partial(kernel, n_exp, n_hid),
        out_shape=[pltpu.VMEM(*k) for k in kept],
        in_specs=[any_spec] * 6,
        out_specs=[vmem_spec] * 8,
        scratch_shapes=[
            pltpu.VMEM((m, d), BF),
            pltpu.VMEM((m, d), BF),
            pltpu.VMEM((d, f), BF),
            pltpu.VMEM((1, f), F32),
            pltpu.VMEM((f, d), BF),
            pltpu.VMEM((f, d), BF),
            pltpu.VMEM((d, f), BF),
            pltpu.VMEM((n_exp * period, LANES), F32),
            pltpu.VMEM((n_exp, period, LANES), BF),
            pltpu.VMEM((n, period, LANES), BF),
            pltpu.VMEM((n * period, LANES), F32),
            pltpu.VMEM((n, period, LANES), BF),
            pltpu.VMEM((n, period, LANES), BF),
            pltpu.SemaphoreType.DMA((6,)),
            pltpu.SemaphoreType.DMA((2,)),
            pltpu.SemaphoreType.DMA((len(batch_cuts(n_exp)),)),
        ],
        compiler_params=pltpu.CompilerParams(
            collective_id=0, has_side_effects=True, vmem_limit_bytes=grant
        ),
        name="soft_moe",
    )(tokens, router.T, w_in, b_in, w_out, cotangent)
    return tuple(
        pl.pallas_call(
            finish,
            out_shape=[jax.ShapeDtypeStruct(tokens.shape, BF)] * 2,
            in_specs=[vmem_spec] * 8,
            out_specs=[any_spec] * 2,
            scratch_shapes=[
                pltpu.VMEM((m, d), BF),
                pltpu.VMEM((m, d), BF),
                pltpu.SemaphoreType.DMA((3,)),
            ],
            compiler_params=pltpu.CompilerParams(vmem_limit_bytes=48 << 20),
            name="finish",
        )(*handed)
    )


def solution(mesh):
    sizes = mesh.shape["expert"], mesh.shape["hidden"]
    return jax.shard_map(
        functools.partial(shards, *sizes),
        mesh=mesh,
        in_specs=(
            P(("expert", "hidden"), None, None),
            P(),
            P("expert", None, "hidden"),
            P("expert", "hidden"),
            P("expert", "hidden", None),
            P(("expert", "hidden"), None, None),
        ),
        out_specs=(P(("expert", "hidden"), None, None), P(("expert", "hidden"), None, None)),
        check_vma=False,
    )
```

```python
import functools
import math

import jax
import jax.numpy as jnp
from jax import lax
from jax.experimental import pallas as pl
from jax.experimental.pallas import tpu as pltpu
from jax.sharding import PartitionSpec as P

MESH = pl.DeviceIdType.MESH
BF = jnp.bfloat16
F32 = jnp.float32
LANES = 128
VMEM_BYTES = 67043328
SLACK = 4096
CLIENTS = 2
FIRST = 4


def dot(a, b, ca, cb):
    return lax.dot_general(a, b, (((ca,), (cb,)), ((), ())), preferred_element_type=F32)


def scatter_rows(scr, base, value, period):
    rows, width = value.shape
    for c in range(width // LANES):
        scr[pl.ds(base + c, rows, stride=period), :] = value[:, c * LANES : (c + 1) * LANES]


def gather_rows(scr, base, rows, chunks, period):
    parts = [scr[pl.ds(base + c, rows, stride=period), :] for c in range(chunks)]
    return jnp.concatenate(parts, axis=1)


def each_peer(n_exp, n_hid, my_e, my_h, act):
    def flip(mine, by, size):
        bit, out = 1, mine
        while bit < size:
            out = out + lax.rem(by // bit, 2) * (bit - 2 * bit * lax.rem(mine // bit, 2))
            bit *= 2
        return out

    hids = [flip(my_h, jnp.int32(j), n_hid) for j in range(n_hid)]

    def step(k, carry):
        e = flip(my_e, n_exp - k, n_exp)
        for j in reversed(range(n_hid)):
            act(e, hids[j])
        return carry

    lax.fori_loop(1, n_exp, step, 0, unroll=n_exp <= 8)
    for j in reversed(range(1, n_hid)):
        act(my_e, hids[j])


def each_peer2(n_exp, n_hid, my_e, my_h, act):
    def flip(mine, by, size):
        bit, out = 1, mine
        while bit < size:
            out = out + lax.rem(by // bit, 2) * (bit - 2 * bit * lax.rem(mine // bit, 2))
            bit *= 2
        return out

    for j in reversed(range(n_hid)):
        h = flip(my_h, jnp.int32(j), n_hid)

        def step(k, carry):
            act(flip(my_e, n_exp - k, n_exp), h)
            return carry

        lax.fori_loop(1, n_exp, step, 0, unroll=n_exp <= 8)
        if j > 0:
            act(my_e, h)


def batch_cuts(n_exp, n_hid):
    return (0, n_hid, n_exp * n_hid // 2, n_exp * n_hid)


def kernel(
    n_exp, n_hid,
    tok_hbm, rt_hbm, wi_hbm, bi_hbm, wo_hbm, cot_hbm,
    tok_t, cot_t, rt, dispatch_ref, combine_ref, combine_t, slot_out, slot_grad,
    tok, cot, wi, bi, wo, wi_t, wo_t, scr_a, send_buf, recv, scr_b, out_buf, ret,
    relay, load_sem, send_sem, recv_sem, relay_sem,
):
    n = n_exp * n_hid
    my_e, my_h = lax.axis_index("expert"), lax.axis_index("hidden")
    me = my_e * n_hid + my_h
    width = tok.shape[1]
    chunks = width // LANES
    period = 2 * chunks

    loads = [
        pltpu.make_async_copy(tok_hbm.at[0], tok, load_sem.at[0]),
        pltpu.make_async_copy(rt_hbm, rt, load_sem.at[1]),
        pltpu.make_async_copy(cot_hbm.at[0], cot, load_sem.at[2]),
        pltpu.make_async_copy(wi_hbm.at[0], wi, load_sem.at[3]),
        pltpu.make_async_copy(bi_hbm, bi, load_sem.at[4]),
        pltpu.make_async_copy(wo_hbm.at[0], wo, load_sem.at[5]),
    ]
    for load in loads[:3]:
        load.start()

    cuts = batch_cuts(n_exp, n_hid)
    my_batch = sum((me >= low).astype(jnp.int32) for low in cuts[1:-1])
    barrier = pltpu.get_barrier_semaphore()

    def greets_first(c):
        return functools.reduce(
            jnp.logical_or, [me == p for p in (1 - c, 2 + c, n_hid + c, 2 * n_hid + c)]
        )

    def greet(k, _):
        dest = lax.rem(me + k, n)

        @pl.when(jnp.logical_or(dest >= CLIENTS, greets_first(dest)))
        def _():
            pl.semaphore_signal(
                barrier, inc=1, device_id=(dest // n_hid, lax.rem(dest, n_hid)), device_id_type=MESH
            )

        return 0

    lax.fori_loop(1, n, greet, 0, unroll=n <= 32)
    for load in loads[3:]:
        load.start()

    loads[0].wait()
    loads[1].wait()
    rt_t = rt[...]
    logits = dot(rt_t, tok[...], 1, 1)
    up = jnp.exp(logits - jnp.max(logits, axis=1, keepdims=True))
    dispatch = up / jnp.sum(up, axis=1, keepdims=True)
    up = jnp.exp(logits - jnp.max(logits, axis=0, keepdims=True))
    combine = up / jnp.sum(up, axis=0, keepdims=True)
    dispatch_ref[...] = dispatch
    combine_ref[...] = combine
    dispatch_w = dispatch.astype(BF)
    combine_w = combine.astype(BF)

    scatter_rows(scr_a, 0, dot(dispatch_w, tok[...], 1, 0), period)
    loads[2].wait()
    scatter_rows(scr_a, chunks, dot(combine_w, cot[...], 1, 0), period)
    send_buf[...] = scr_a[...].reshape(send_buf.shape).astype(BF)


    def send_slots(e, h):
        pltpu.make_async_remote_copy(
            src_ref=send_buf.at[e],
            dst_ref=recv.at[me],
            send_sem=send_sem.at[0],
            recv_sem=recv_sem.at[my_batch],
            device_id=(e, h),
            device_id_type=MESH,
        ).start()

    def lend(e, dest):
        pltpu.make_async_remote_copy(
            src_ref=send_buf.at[e],
            dst_ref=relay.at[e],
            send_sem=send_sem.at[0],
            recv_sem=relay_sem.at[0],
            device_id=dest,
            device_id_type=MESH,
        ).start()

    def each(count, act):
        lax.fori_loop(0, count, lambda k, _: (act(k), 0)[1], 0, unroll=count <= 8)

    half = n_exp // 2
    shares = (
        (n_hid, half, lambda k: n_exp - 1 - 2 * k, range(n_hid)),
        (2 * n_hid, half - 1, lambda k: n_exp - 2 - 2 * k, range(n_hid)),
        (2, 1, lambda k: 0 * k, range(2, n_hid)),
    )

    @pl.when(me < CLIENTS)
    def _():
        pl.semaphore_wait(barrier, FIRST)
        for place, count, expert, _ in shares:
            dest = (jnp.int32(place // n_hid), place % n_hid + my_h)
            each(count, lambda k: lend(expert(k), dest))
        send_slots(jnp.int32(0), 1 - my_h)

    @pl.when(me >= CLIENTS)
    def _():
        pl.semaphore_wait(barrier, n - 1)

    for place, count, expert, hiddens in shares:
        client = me - place

        @pl.when(jnp.logical_and(client >= 0, client < CLIENTS))
        def _():
            lent = pl.ds(0, count)
            pltpu.make_async_copy(relay.at[lent], relay.at[lent], relay_sem.at[0]).wait()

            def hand(k):
                for h in reversed(hiddens):

                    @pl.when(expert(k) * n_hid + h != me)
                    def _():
                        pltpu.make_async_remote_copy(
                            src_ref=relay.at[expert(k)],
                            dst_ref=recv.at[client],
                            send_sem=relay_sem.at[1],
                            recv_sem=recv_sem.at[0],
                            device_id=(jnp.int32(0) + expert(k), jnp.int32(h)),
                            device_id_type=MESH,
                        ).start()

            each(count, hand)
            pltpu.make_async_copy(relay.at[my_e], recv.at[client], recv_sem.at[0]).start()

    @pl.when(me >= CLIENTS)
    def _():
        each_peer(n_exp, n_hid, my_e, my_h, send_slots)

    pltpu.make_async_copy(send_buf.at[my_e], recv.at[me], recv_sem.at[my_batch]).start()

    combine_t[...] = combine.T.astype(BF)
    for i in (3, 4, 5):
        loads[i].wait()
    wi_t[...] = wi[...].T
    wo_t[...] = wo[...].T
    tok_t[...] = tok[...].T
    cot_t[...] = cot[...].T

    scale, cubic = math.sqrt(2.0 / math.pi), 0.044715
    others = pl.ds(0, n - 1)
    back_sem = len(cuts) - 1
    for b, (low, high) in enumerate(zip(cuts, cuts[1:])):
        first, rows = low, high - low
        span = pl.ds(first, rows)
        pltpu.make_async_copy(recv.at[span], recv.at[span], recv_sem.at[b]).wait()
        if b == 0:
            for c in range(CLIENTS):

                @pl.when(jnp.logical_not(jnp.logical_or(greets_first(c), me == c)))
                def _():
                    pl.semaphore_signal(
                        barrier, inc=1, device_id=(jnp.int32(0), jnp.int32(c)), device_id_type=MESH
                    )


        base = first * period
        scr_b[pl.ds(base, rows * period), :] = recv[span].astype(F32).reshape(rows * period, LANES)
        rows_in = gather_rows(scr_b, base, rows, chunks, period).astype(BF)
        rows_cot = gather_rows(scr_b, base + chunks, rows, chunks, period).astype(BF)
        pre = dot(rows_in, wi[...], 1, 0) + bi[...]
        act_grad = dot(rows_cot, wo_t[...], 1, 0)
        square = pre * pre
        tanh = jnp.tanh(scale * (pre + cubic * (square * pre)))
        cdf = 0.5 * (1.0 + tanh)
        act = (pre * cdf).astype(BF)
        slope = cdf + 0.5 * pre * (1.0 - tanh * tanh) * (scale * (1.0 + (3.0 * cubic) * square))
        pre_grad = (act_grad * slope).astype(BF)
        scatter_rows(scr_b, base, dot(act, wo[...], 1, 0), period)
        scatter_rows(scr_b, base + chunks, dot(pre_grad, wi_t[...], 1, 0), period)
        out_buf[span] = scr_b[pl.ds(base, rows * period), :].reshape((rows,) + out_buf.shape[1:]).astype(BF)

        def send_to(e, h):
            pltpu.make_async_remote_copy(
                src_ref=out_buf.at[e * n_hid + h],
                dst_ref=ret.at[me],
                send_sem=send_sem.at[1],
                recv_sem=recv_sem.at[back_sem],
                device_id=(e, h),
                device_id_type=MESH,
            ).start()

        def send_back(e, h):
            @pl.when(jnp.logical_and(e >= low, e < high))
            def _():
                pltpu.make_async_remote_copy(
                    src_ref=out_buf.at[e * n_hid + h],
                    dst_ref=ret.at[me],
                    send_sem=send_sem.at[1],
                    recv_sem=recv_sem.at[back_sem],
                    device_id=(e, h),
                    device_id_type=MESH,
                ).start()

        def send_batch(low, high):
            for dest in range(low, high):

                @pl.when(me != dest)
                def _():
                    send_to(jnp.int32(dest // n_hid), jnp.int32(dest % n_hid))

        if b < len(cuts) - 2:

            @pl.when(me >= CLIENTS)
            def _():
                send_batch(low, high)

        else:

            @pl.when(me < CLIENTS)
            def _():
                pl.semaphore_wait(barrier, n - 1 - FIRST)
                send_batch(0, low)

            def send_back(e, h):
                @pl.when(e * n_hid + h >= low)
                def _():
                    send_to(e, h)

            each_peer2(n_exp, n_hid, my_e, my_h, send_back)
    ret[me] = out_buf[me]
    pltpu.make_async_copy(ret.at[others], ret.at[others], recv_sem.at[back_sem]).wait()

    total = jnp.sum(ret[...].astype(F32).reshape((n_exp, n_hid) + ret.shape[1:]), axis=1)
    scr_a[...] = total.reshape(scr_a.shape)
    slot_out[...] = gather_rows(scr_a, 0, n_exp, chunks, period).astype(BF)
    slot_grad[...] = gather_rows(scr_a, chunks, n_exp, chunks, period).astype(BF)

    def sent(count, sem):
        span = pl.ds(0, count)
        pltpu.make_async_copy(out_buf.at[span], out_buf.at[span], sem).wait()

    @pl.when(me < CLIENTS)
    def _():
        sent(n_exp + 1, send_sem.at[0])

    @pl.when(me >= CLIENTS)
    def _():
        sent(n - 1, send_sem.at[0])

    for place, count, _, hiddens in shares:

        @pl.when(jnp.logical_and(me >= place, me < place + CLIENTS))
        def _():
            sent(count * len(hiddens) - 1, relay_sem.at[1])

    sent(n - 1, send_sem.at[1])


def finish(tok_t, cot_t, rt, dispatch_ref, combine_ref, combine_t, slot_out, slot_grad,
           mixed_hbm, grad_hbm, mixed_v, grad_v, out_sem):
    dispatch, combine = dispatch_ref[...], combine_ref[...]
    mixed_v[...] = dot(combine_t[...], slot_out[...], 1, 0).astype(BF)
    put_mixed = pltpu.make_async_copy(mixed_v, mixed_hbm.at[0], out_sem.at[0])
    put_mixed.start()
    combine_grad = dot(slot_out[...], cot_t[...], 1, 0)
    dispatch_grad = dot(slot_grad[...], tok_t[...], 1, 0)
    logit_grad = combine * (combine_grad - jnp.sum(combine * combine_grad, axis=0, keepdims=True))
    logit_grad = logit_grad + dispatch * (
        dispatch_grad - jnp.sum(dispatch * dispatch_grad, axis=1, keepdims=True)
    )
    left = jnp.concatenate([dispatch, logit_grad], axis=0).T.astype(BF)
    right = jnp.concatenate([slot_grad[...], rt[...]], axis=0)
    tokens = left.shape[0]
    half = -(-tokens // 32) * 16
    puts = [put_mixed]
    for i, (low, size) in enumerate(((0, half), (half, tokens - half))):
        span = pl.ds(low, size)
        grad_v[span, :] = dot(left[low : low + size], right, 1, 0).astype(BF)
        put = pltpu.make_async_copy(grad_v.at[span], grad_hbm.at[0, span], out_sem.at[1 + i])
        put.start()
        puts.append(put)
    for put in puts:
        put.wait()


def shards(n_exp, n_hid, tokens, router, w_in, b_in, w_out, cotangent):
    n = n_exp * n_hid
    _, m, d = tokens.shape
    f = w_in.shape[2]
    period = 2 * d // LANES
    assert tokens.shape[0] == 1 and w_in.shape[0] == 1
    any_spec = pl.BlockSpec(memory_space=pl.ANY)
    vmem_spec = pl.BlockSpec(memory_space=pltpu.VMEM)
    kept = [((d, m), BF)] * 2 + [((n_exp, d), BF)] + [((n_exp, m), F32)] * 2 + [((m, n_exp), BF)] + [((n_exp, d), BF)] * 2
    held = sum(-(-r // 8) * 8 * -(-c // LANES) * LANES * jnp.dtype(t).itemsize for (r, c), t in kept)
    grant = VMEM_BYTES - held - SLACK
    handed = pl.pallas_call(
        functools.partial(kernel, n_exp, n_hid),
        out_shape=[pltpu.VMEM(*k) for k in kept],
        in_specs=[any_spec] * 6,
        out_specs=[vmem_spec] * 8,
        scratch_shapes=[
            pltpu.VMEM((m, d), BF),
            pltpu.VMEM((m, d), BF),
            pltpu.VMEM((d, f), BF),
            pltpu.VMEM((1, f), F32),
            pltpu.VMEM((f, d), BF),
            pltpu.VMEM((f, d), BF),
            pltpu.VMEM((d, f), BF),
            pltpu.VMEM((n_exp * period, LANES), F32),
            pltpu.VMEM((n_exp, period, LANES), BF),
            pltpu.VMEM((n, period, LANES), BF),
            pltpu.VMEM((n * period, LANES), F32),
            pltpu.VMEM((n, period, LANES), BF),
            pltpu.VMEM((n, period, LANES), BF),
            pltpu.VMEM((n_exp, period, LANES), BF),
            pltpu.SemaphoreType.DMA((6,)),
            pltpu.SemaphoreType.DMA((2,)),
            pltpu.SemaphoreType.DMA((len(batch_cuts(n_exp, n_hid)),)),
            pltpu.SemaphoreType.DMA((2,)),
        ],
        compiler_params=pltpu.CompilerParams(
            collective_id=0, has_side_effects=True, vmem_limit_bytes=grant
        ),
        name="soft_moe",
    )(tokens, router.T, w_in, b_in, w_out, cotangent)
    return tuple(
        pl.pallas_call(
            finish,
            out_shape=[jax.ShapeDtypeStruct(tokens.shape, BF)] * 2,
            in_specs=[vmem_spec] * 8,
            out_specs=[any_spec] * 2,
            scratch_shapes=[
                pltpu.VMEM((m, d), BF),
                pltpu.VMEM((m, d), BF),
                pltpu.SemaphoreType.DMA((3,)),
            ],
            compiler_params=pltpu.CompilerParams(vmem_limit_bytes=48 << 20),
            name="finish",
        )(*handed)
    )


def solution(mesh):
    sizes = mesh.shape["expert"], mesh.shape["hidden"]
    return jax.shard_map(
        functools.partial(shards, *sizes),
        mesh=mesh,
        in_specs=(
            P(("expert", "hidden"), None, None),
            P(),
            P("expert", None, "hidden"),
            P("expert", "hidden"),
            P("expert", "hidden", None),
            P(("expert", "hidden"), None, None),
        ),
        out_specs=(P(("expert", "hidden"), None, None), P(("expert", "hidden"), None, None)),
        check_vma=False,
    )
```

```python
import functools
import math

import jax
import jax.numpy as jnp
from jax import lax
from jax.experimental import pallas as pl
from jax.experimental.pallas import tpu as pltpu
from jax.sharding import PartitionSpec as P

MESH = pl.DeviceIdType.MESH
BF = jnp.bfloat16
F32 = jnp.float32
LANES = 128
VMEM_BYTES = 67043328
SLACK = 4096
CLIENTS = 2
FIRST = 4


def dot(a, b, ca, cb):
    return lax.dot_general(a, b, (((ca,), (cb,)), ((), ())), preferred_element_type=F32)


def scatter_rows(scr, base, value, period):
    rows, width = value.shape
    for c in range(width // LANES):
        scr[pl.ds(base + c, rows, stride=period), :] = value[:, c * LANES : (c + 1) * LANES]


def gather_rows(scr, base, rows, chunks, period):
    parts = [scr[pl.ds(base + c, rows, stride=period), :] for c in range(chunks)]
    return jnp.concatenate(parts, axis=1)


def each_peer(n_exp, n_hid, my_e, my_h, act):
    def flip(mine, by, size):
        bit, out = 1, mine
        while bit < size:
            out = out + lax.rem(by // bit, 2) * (bit - 2 * bit * lax.rem(mine // bit, 2))
            bit *= 2
        return out

    hids = [flip(my_h, jnp.int32(j), n_hid) for j in range(n_hid)]

    def step(k, carry):
        e = flip(my_e, n_exp - k, n_exp)
        for j in reversed(range(n_hid)):
            act(e, hids[j])
        return carry

    lax.fori_loop(1, n_exp, step, 0, unroll=n_exp <= 8)
    for j in reversed(range(1, n_hid)):
        act(my_e, hids[j])


def each_peer2(n_exp, n_hid, my_e, my_h, act):
    def flip(mine, by, size):
        bit, out = 1, mine
        while bit < size:
            out = out + lax.rem(by // bit, 2) * (bit - 2 * bit * lax.rem(mine // bit, 2))
            bit *= 2
        return out

    for j in reversed(range(n_hid)):
        h = flip(my_h, jnp.int32(j), n_hid)

        def step(k, carry):
            act(flip(my_e, n_exp - k, n_exp), h)
            return carry

        lax.fori_loop(1, n_exp, step, 0, unroll=n_exp <= 8)
        if j > 0:
            act(my_e, h)


def batch_cuts(n_exp, n_hid):
    return (0, 2, 2 * n_hid, n_exp * n_hid)


def kernel(
    n_exp, n_hid,
    tok_hbm, rt_hbm, wi_hbm, bi_hbm, wo_hbm, cot_hbm,
    tok_t, cot_t, rt, dispatch_ref, combine_ref, combine_t, slot_out, slot_grad,
    tok, cot, wi, bi, wo, wi_t, wo_t, scr_a, send_buf, recv, scr_b, out_buf, ret,
    relay, load_sem, send_sem, recv_sem, relay_sem,
):
    n = n_exp * n_hid
    my_e, my_h = lax.axis_index("expert"), lax.axis_index("hidden")
    me = my_e * n_hid + my_h
    width = tok.shape[1]
    chunks = width // LANES
    period = 2 * chunks

    loads = [
        pltpu.make_async_copy(tok_hbm.at[0], tok, load_sem.at[0]),
        pltpu.make_async_copy(rt_hbm, rt, load_sem.at[1]),
        pltpu.make_async_copy(cot_hbm.at[0], cot, load_sem.at[2]),
        pltpu.make_async_copy(wi_hbm.at[0], wi, load_sem.at[3]),
        pltpu.make_async_copy(bi_hbm, bi, load_sem.at[4]),
        pltpu.make_async_copy(wo_hbm.at[0], wo, load_sem.at[5]),
    ]
    for load in loads[:3]:
        load.start()

    cuts = batch_cuts(n_exp, n_hid)
    my_batch = sum((me >= low).astype(jnp.int32) for low in cuts[1:-1])
    barrier = pltpu.get_barrier_semaphore()

    def greets_first(c):
        return functools.reduce(
            jnp.logical_or, [me == p for p in (1 - c, 2 + c, n_hid + c, 2 * n_hid + c)]
        )

    def greet(k, _):
        dest = lax.rem(me + k, n)

        @pl.when(jnp.logical_or(dest >= CLIENTS, greets_first(dest)))
        def _():
            pl.semaphore_signal(
                barrier, inc=1, device_id=(dest // n_hid, lax.rem(dest, n_hid)), device_id_type=MESH
            )

        return 0

    lax.fori_loop(1, n, greet, 0, unroll=n <= 32)
    for load in loads[3:]:
        load.start()

    loads[0].wait()
    loads[1].wait()
    rt_t = rt[...]
    logits = dot(rt_t, tok[...], 1, 1)
    up = jnp.exp(logits - jnp.max(logits, axis=1, keepdims=True))
    dispatch = up / jnp.sum(up, axis=1, keepdims=True)
    up = jnp.exp(logits - jnp.max(logits, axis=0, keepdims=True))
    combine = up / jnp.sum(up, axis=0, keepdims=True)
    dispatch_ref[...] = dispatch
    combine_ref[...] = combine
    dispatch_w = dispatch.astype(BF)
    combine_w = combine.astype(BF)

    scatter_rows(scr_a, 0, dot(dispatch_w, tok[...], 1, 0), period)
    loads[2].wait()
    scatter_rows(scr_a, chunks, dot(combine_w, cot[...], 1, 0), period)
    send_buf[...] = scr_a[...].reshape(send_buf.shape).astype(BF)


    def send_slots(e, h):
        pltpu.make_async_remote_copy(
            src_ref=send_buf.at[e],
            dst_ref=recv.at[me],
            send_sem=send_sem.at[0],
            recv_sem=recv_sem.at[my_batch],
            device_id=(e, h),
            device_id_type=MESH,
        ).start()

    def lend(e, dest):
        pltpu.make_async_remote_copy(
            src_ref=send_buf.at[e],
            dst_ref=relay.at[e],
            send_sem=send_sem.at[0],
            recv_sem=relay_sem.at[0],
            device_id=dest,
            device_id_type=MESH,
        ).start()

    def each(count, act):
        lax.fori_loop(0, count, lambda k, _: (act(k), 0)[1], 0, unroll=count <= 8)

    half = n_exp // 2
    shares = (
        (2, half + 1, lambda k: jnp.maximum(n_exp - 1 - 2 * k, 0), range(2, n_hid)),
        (n_hid, half, lambda k: n_exp - 1 - 2 * k, range(2)),
        (2 * n_hid, half - 1, lambda k: n_exp - 2 - 2 * k, range(n_hid)),
    )

    @pl.when(me < CLIENTS)
    def _():
        pl.semaphore_wait(barrier, FIRST)
        for place, count, expert, _ in shares:
            dest = (jnp.int32(place // n_hid), place % n_hid + my_h)
            each(count, lambda k: lend(expert(k), dest))
        send_slots(jnp.int32(0), 1 - my_h)

    @pl.when(me >= CLIENTS)
    def _():
        pl.semaphore_wait(barrier, n - 1)

    for place, count, expert, hiddens in shares:
        client = me - place

        @pl.when(jnp.logical_and(client >= 0, client < CLIENTS))
        def _():
            lent = pl.ds(0, count)
            pltpu.make_async_copy(relay.at[lent], relay.at[lent], relay_sem.at[0]).wait()

            def hand(k):
                for h in reversed(hiddens):

                    @pl.when(expert(k) * n_hid + h != me)
                    def _():
                        pltpu.make_async_remote_copy(
                            src_ref=relay.at[expert(k)],
                            dst_ref=recv.at[client],
                            send_sem=relay_sem.at[1],
                            recv_sem=recv_sem.at[0],
                            device_id=(jnp.int32(0) + expert(k), jnp.int32(h)),
                            device_id_type=MESH,
                        ).start()

            each(count, hand)
            pltpu.make_async_copy(relay.at[my_e], recv.at[client], recv_sem.at[0]).start()

    @pl.when(me >= CLIENTS)
    def _():
        each_peer(n_exp, n_hid, my_e, my_h, send_slots)

    pltpu.make_async_copy(send_buf.at[my_e], recv.at[me], recv_sem.at[my_batch]).start()

    combine_t[...] = combine.T.astype(BF)
    for i in (3, 4, 5):
        loads[i].wait()
    wi_t[...] = wi[...].T
    wo_t[...] = wo[...].T
    tok_t[...] = tok[...].T
    cot_t[...] = cot[...].T

    scale, cubic = math.sqrt(2.0 / math.pi), 0.044715
    others = pl.ds(0, n - 1)
    back_sem = len(cuts) - 1
    for b, (low, high) in enumerate(zip(cuts, cuts[1:])):
        first, rows = low, high - low
        span = pl.ds(first, rows)
        pltpu.make_async_copy(recv.at[span], recv.at[span], recv_sem.at[b]).wait()
        if b == 0:
            for c in range(CLIENTS):

                @pl.when(jnp.logical_not(jnp.logical_or(greets_first(c), me == c)))
                def _():
                    pl.semaphore_signal(
                        barrier, inc=1, device_id=(jnp.int32(0), jnp.int32(c)), device_id_type=MESH
                    )


        base = first * period
        scr_b[pl.ds(base, rows * period), :] = recv[span].astype(F32).reshape(rows * period, LANES)
        rows_in = gather_rows(scr_b, base, rows, chunks, period).astype(BF)
        rows_cot = gather_rows(scr_b, base + chunks, rows, chunks, period).astype(BF)
        pre = dot(rows_in, wi[...], 1, 0) + bi[...]
        act_grad = dot(rows_cot, wo_t[...], 1, 0)
        square = pre * pre
        tanh = jnp.tanh(scale * (pre + cubic * (square * pre)))
        cdf = 0.5 * (1.0 + tanh)
        act = (pre * cdf).astype(BF)
        slope = cdf + 0.5 * pre * (1.0 - tanh * tanh) * (scale * (1.0 + (3.0 * cubic) * square))
        pre_grad = (act_grad * slope).astype(BF)
        scatter_rows(scr_b, base, dot(act, wo[...], 1, 0), period)
        scatter_rows(scr_b, base + chunks, dot(pre_grad, wi_t[...], 1, 0), period)
        out_buf[span] = scr_b[pl.ds(base, rows * period), :].reshape((rows,) + out_buf.shape[1:]).astype(BF)

        def send_to(e, h):
            pltpu.make_async_remote_copy(
                src_ref=out_buf.at[e * n_hid + h],
                dst_ref=ret.at[me],
                send_sem=send_sem.at[1],
                recv_sem=recv_sem.at[back_sem],
                device_id=(e, h),
                device_id_type=MESH,
            ).start()

        def send_back(e, h):
            @pl.when(jnp.logical_and(e >= low, e < high))
            def _():
                pltpu.make_async_remote_copy(
                    src_ref=out_buf.at[e * n_hid + h],
                    dst_ref=ret.at[me],
                    send_sem=send_sem.at[1],
                    recv_sem=recv_sem.at[back_sem],
                    device_id=(e, h),
                    device_id_type=MESH,
                ).start()

        def send_batch(low, high):
            for dest in range(low, high):

                @pl.when(me != dest)
                def _():
                    send_to(jnp.int32(dest // n_hid), jnp.int32(dest % n_hid))

        if b < len(cuts) - 2:

            @pl.when(me >= CLIENTS)
            def _():
                send_batch(low, high)

        else:

            @pl.when(me < CLIENTS)
            def _():
                pl.semaphore_wait(barrier, n - 1 - FIRST)
                send_batch(0, low)

            def send_back(e, h):
                @pl.when(e * n_hid + h >= low)
                def _():
                    send_to(e, h)

            each_peer2(n_exp, n_hid, my_e, my_h, send_back)
    ret[me] = out_buf[me]
    pltpu.make_async_copy(ret.at[others], ret.at[others], recv_sem.at[back_sem]).wait()

    total = jnp.sum(ret[...].astype(F32).reshape((n_exp, n_hid) + ret.shape[1:]), axis=1)
    scr_a[...] = total.reshape(scr_a.shape)
    slot_out[...] = gather_rows(scr_a, 0, n_exp, chunks, period).astype(BF)
    slot_grad[...] = gather_rows(scr_a, chunks, n_exp, chunks, period).astype(BF)

    def sent(count, sem):
        span = pl.ds(0, count)
        pltpu.make_async_copy(out_buf.at[span], out_buf.at[span], sem).wait()

    @pl.when(me < CLIENTS)
    def _():
        sent(sum(count for _, count, _, _ in shares) + 1, send_sem.at[0])

    @pl.when(me >= CLIENTS)
    def _():
        sent(n - 1, send_sem.at[0])

    for place, count, _, hiddens in shares:

        @pl.when(jnp.logical_and(me >= place, me < place + CLIENTS))
        def _():
            sent(count * len(hiddens) - 1, relay_sem.at[1])

    sent(n - 1, send_sem.at[1])


def finish(tok_t, cot_t, rt, dispatch_ref, combine_ref, combine_t, slot_out, slot_grad,
           mixed_hbm, grad_hbm, mixed_v, grad_v, out_sem):
    dispatch, combine = dispatch_ref[...], combine_ref[...]
    mixed_v[...] = dot(combine_t[...], slot_out[...], 1, 0).astype(BF)
    put_mixed = pltpu.make_async_copy(mixed_v, mixed_hbm.at[0], out_sem.at[0])
    put_mixed.start()
    combine_grad = dot(slot_out[...], cot_t[...], 1, 0)
    dispatch_grad = dot(slot_grad[...], tok_t[...], 1, 0)
    logit_grad = combine * (combine_grad - jnp.sum(combine * combine_grad, axis=0, keepdims=True))
    logit_grad = logit_grad + dispatch * (
        dispatch_grad - jnp.sum(dispatch * dispatch_grad, axis=1, keepdims=True)
    )
    left = jnp.concatenate([dispatch, logit_grad], axis=0).T.astype(BF)
    right = jnp.concatenate([slot_grad[...], rt[...]], axis=0)
    tokens = left.shape[0]
    half = -(-tokens // 32) * 16
    puts = [put_mixed]
    for i, (low, size) in enumerate(((0, half), (half, tokens - half))):
        span = pl.ds(low, size)
        grad_v[span, :] = dot(left[low : low + size], right, 1, 0).astype(BF)
        put = pltpu.make_async_copy(grad_v.at[span], grad_hbm.at[0, span], out_sem.at[1 + i])
        put.start()
        puts.append(put)
    for put in puts:
        put.wait()


def shards(n_exp, n_hid, tokens, router, w_in, b_in, w_out, cotangent):
    n = n_exp * n_hid
    _, m, d = tokens.shape
    f = w_in.shape[2]
    period = 2 * d // LANES
    assert tokens.shape[0] == 1 and w_in.shape[0] == 1
    any_spec = pl.BlockSpec(memory_space=pl.ANY)
    vmem_spec = pl.BlockSpec(memory_space=pltpu.VMEM)
    kept = [((d, m), BF)] * 2 + [((n_exp, d), BF)] + [((n_exp, m), F32)] * 2 + [((m, n_exp), BF)] + [((n_exp, d), BF)] * 2
    held = sum(-(-r // 8) * 8 * -(-c // LANES) * LANES * jnp.dtype(t).itemsize for (r, c), t in kept)
    grant = VMEM_BYTES - held - SLACK
    handed = pl.pallas_call(
        functools.partial(kernel, n_exp, n_hid),
        out_shape=[pltpu.VMEM(*k) for k in kept],
        in_specs=[any_spec] * 6,
        out_specs=[vmem_spec] * 8,
        scratch_shapes=[
            pltpu.VMEM((m, d), BF),
            pltpu.VMEM((m, d), BF),
            pltpu.VMEM((d, f), BF),
            pltpu.VMEM((1, f), F32),
            pltpu.VMEM((f, d), BF),
            pltpu.VMEM((f, d), BF),
            pltpu.VMEM((d, f), BF),
            pltpu.VMEM((n_exp * period, LANES), F32),
            pltpu.VMEM((n_exp, period, LANES), BF),
            pltpu.VMEM((n, period, LANES), BF),
            pltpu.VMEM((n * period, LANES), F32),
            pltpu.VMEM((n, period, LANES), BF),
            pltpu.VMEM((n, period, LANES), BF),
            pltpu.VMEM((n_exp, period, LANES), BF),
            pltpu.SemaphoreType.DMA((6,)),
            pltpu.SemaphoreType.DMA((2,)),
            pltpu.SemaphoreType.DMA((len(batch_cuts(n_exp, n_hid)),)),
            pltpu.SemaphoreType.DMA((2,)),
        ],
        compiler_params=pltpu.CompilerParams(
            collective_id=0, has_side_effects=True, vmem_limit_bytes=grant
        ),
        name="soft_moe",
    )(tokens, router.T, w_in, b_in, w_out, cotangent)
    return tuple(
        pl.pallas_call(
            finish,
            out_shape=[jax.ShapeDtypeStruct(tokens.shape, BF)] * 2,
            in_specs=[vmem_spec] * 8,
            out_specs=[any_spec] * 2,
            scratch_shapes=[
                pltpu.VMEM((m, d), BF),
                pltpu.VMEM((m, d), BF),
                pltpu.SemaphoreType.DMA((3,)),
            ],
            compiler_params=pltpu.CompilerParams(vmem_limit_bytes=48 << 20),
            name="finish",
        )(*handed)
    )


def solution(mesh):
    sizes = mesh.shape["expert"], mesh.shape["hidden"]
    return jax.shard_map(
        functools.partial(shards, *sizes),
        mesh=mesh,
        in_specs=(
            P(("expert", "hidden"), None, None),
            P(),
            P("expert", None, "hidden"),
            P("expert", "hidden"),
            P("expert", "hidden", None),
            P(("expert", "hidden"), None, None),
        ),
        out_specs=(P(("expert", "hidden"), None, None), P(("expert", "hidden"), None, None)),
        check_vma=False,
    )
```

```python
import functools
import math

import jax
import jax.numpy as jnp
from jax import lax
from jax.experimental import pallas as pl
from jax.experimental.pallas import tpu as pltpu
from jax.sharding import PartitionSpec as P

MESH = pl.DeviceIdType.MESH
BF = jnp.bfloat16
F32 = jnp.float32
LANES = 128
VMEM_BYTES = 67043328
SLACK = 4096
CLIENTS = 2
FIRST = 4


def dot(a, b, ca, cb):
    return lax.dot_general(a, b, (((ca,), (cb,)), ((), ())), preferred_element_type=F32)


def scatter_rows(scr, base, value, period):
    rows, width = value.shape
    for c in range(width // LANES):
        scr[pl.ds(base + c, rows, stride=period), :] = value[:, c * LANES : (c + 1) * LANES]


def gather_rows(scr, base, rows, chunks, period):
    parts = [scr[pl.ds(base + c, rows, stride=period), :] for c in range(chunks)]
    return jnp.concatenate(parts, axis=1)


def each_peer(n_exp, n_hid, my_e, my_h, act):
    def flip(mine, by, size):
        bit, out = 1, mine
        while bit < size:
            out = out + lax.rem(by // bit, 2) * (bit - 2 * bit * lax.rem(mine // bit, 2))
            bit *= 2
        return out

    hids = [flip(my_h, jnp.int32(j), n_hid) for j in range(n_hid)]

    def step(k, carry):
        e = flip(my_e, n_exp - k, n_exp)
        for j in reversed(range(n_hid)):
            act(e, hids[j])
        return carry

    lax.fori_loop(1, n_exp, step, 0, unroll=n_exp <= 8)
    for j in reversed(range(1, n_hid)):
        act(my_e, hids[j])


def each_peer2(n_exp, n_hid, my_e, my_h, act):
    def flip(mine, by, size):
        bit, out = 1, mine
        while bit < size:
            out = out + lax.rem(by // bit, 2) * (bit - 2 * bit * lax.rem(mine // bit, 2))
            bit *= 2
        return out

    for j in reversed(range(n_hid)):
        h = flip(my_h, jnp.int32(j), n_hid)

        def step(k, carry):
            act(flip(my_e, n_exp - k, n_exp), h)
            return carry

        lax.fori_loop(1, n_exp, step, 0, unroll=n_exp <= 8)
        if j > 0:
            act(my_e, h)


def slot_of(i, n):
    last = i >= n - n // 4
    return jnp.where(last, i - n // 2, jnp.where(i >= n // 4, i + n // 4, i))


def batch_cuts(n_exp, n_hid):
    return (0, 2, n_exp * n_hid // 2, n_exp * n_hid)


def kernel(
    n_exp, n_hid,
    tok_hbm, rt_hbm, wi_hbm, bi_hbm, wo_hbm, cot_hbm,
    tok_t, cot_t, rt, dispatch_ref, combine_ref, combine_t, slot_out, slot_grad,
    tok, cot, wi, bi, wo, wi_t, wo_t, scr_a, send_buf, recv, scr_b, out_buf, ret,
    relay, load_sem, send_sem, recv_sem, relay_sem,
):
    n = n_exp * n_hid
    my_e, my_h = lax.axis_index("expert"), lax.axis_index("hidden")
    me = my_e * n_hid + my_h
    width = tok.shape[1]
    chunks = width // LANES
    period = 2 * chunks

    loads = [
        pltpu.make_async_copy(tok_hbm.at[0], tok, load_sem.at[0]),
        pltpu.make_async_copy(rt_hbm, rt, load_sem.at[1]),
        pltpu.make_async_copy(cot_hbm.at[0], cot, load_sem.at[2]),
        pltpu.make_async_copy(wi_hbm.at[0], wi, load_sem.at[3]),
        pltpu.make_async_copy(bi_hbm, bi, load_sem.at[4]),
        pltpu.make_async_copy(wo_hbm.at[0], wo, load_sem.at[5]),
    ]
    for load in loads[:3]:
        load.start()

    cuts = batch_cuts(n_exp, n_hid)
    slot = slot_of(me, n)
    my_batch = sum((slot >= low).astype(jnp.int32) for low in cuts[1:-1])
    barrier = pltpu.get_barrier_semaphore()

    def greets_first(c):
        return functools.reduce(
            jnp.logical_or, [me == p for p in (1 - c, 2 + c, n_hid + c, 2 * n_hid + c)]
        )

    def greet(k, _):
        dest = lax.rem(me + k, n)

        @pl.when(jnp.logical_or(dest >= CLIENTS, greets_first(dest)))
        def _():
            pl.semaphore_signal(
                barrier, inc=1, device_id=(dest // n_hid, lax.rem(dest, n_hid)), device_id_type=MESH
            )

        return 0

    lax.fori_loop(1, n, greet, 0, unroll=n <= 32)
    for load in loads[3:]:
        load.start()

    loads[0].wait()
    loads[1].wait()
    rt_t = rt[...]
    logits = dot(rt_t, tok[...], 1, 1)
    up = jnp.exp(logits - jnp.max(logits, axis=1, keepdims=True))
    dispatch = up / jnp.sum(up, axis=1, keepdims=True)
    up = jnp.exp(logits - jnp.max(logits, axis=0, keepdims=True))
    combine = up / jnp.sum(up, axis=0, keepdims=True)
    dispatch_ref[...] = dispatch
    combine_ref[...] = combine
    dispatch_w = dispatch.astype(BF)
    combine_w = combine.astype(BF)

    scatter_rows(scr_a, 0, dot(dispatch_w, tok[...], 1, 0), period)
    loads[2].wait()
    scatter_rows(scr_a, chunks, dot(combine_w, cot[...], 1, 0), period)
    send_buf[...] = scr_a[...].reshape(send_buf.shape).astype(BF)


    def send_slots(e, h):
        pltpu.make_async_remote_copy(
            src_ref=send_buf.at[e],
            dst_ref=recv.at[slot],
            send_sem=send_sem.at[0],
            recv_sem=recv_sem.at[my_batch],
            device_id=(e, h),
            device_id_type=MESH,
        ).start()

    def lend(e, dest):
        pltpu.make_async_remote_copy(
            src_ref=send_buf.at[e],
            dst_ref=relay.at[e],
            send_sem=send_sem.at[0],
            recv_sem=relay_sem.at[0],
            device_id=dest,
            device_id_type=MESH,
        ).start()

    def each(count, act):
        lax.fori_loop(0, count, lambda k, _: (act(k), 0)[1], 0, unroll=count <= 8)

    half = n_exp // 2
    shares = (
        (2, half + 1, lambda k: jnp.maximum(n_exp - 1 - 2 * k, 0), range(2, n_hid)),
        (n_hid, half, lambda k: n_exp - 1 - 2 * k, range(2)),
        (2 * n_hid, half - 1, lambda k: n_exp - 2 - 2 * k, range(n_hid)),
    )

    @pl.when(me < CLIENTS)
    def _():
        pl.semaphore_wait(barrier, FIRST)
        for place, count, expert, _ in shares:
            dest = (jnp.int32(place // n_hid), place % n_hid + my_h)
            each(count, lambda k: lend(expert(k), dest))
        send_slots(jnp.int32(0), 1 - my_h)

    @pl.when(me >= CLIENTS)
    def _():
        pl.semaphore_wait(barrier, n - 1)

    for place, count, expert, hiddens in shares:
        client = me - place

        @pl.when(jnp.logical_and(client >= 0, client < CLIENTS))
        def _():
            lent = pl.ds(0, count)
            pltpu.make_async_copy(relay.at[lent], relay.at[lent], relay_sem.at[0]).wait()

            def hand(k):
                for h in reversed(hiddens):

                    @pl.when(expert(k) * n_hid + h != me)
                    def _():
                        pltpu.make_async_remote_copy(
                            src_ref=relay.at[expert(k)],
                            dst_ref=recv.at[client],
                            send_sem=relay_sem.at[1],
                            recv_sem=recv_sem.at[0],
                            device_id=(jnp.int32(0) + expert(k), jnp.int32(h)),
                            device_id_type=MESH,
                        ).start()

            each(count, hand)
            pltpu.make_async_copy(relay.at[my_e], recv.at[client], recv_sem.at[0]).start()

    @pl.when(me >= CLIENTS)
    def _():
        each_peer(n_exp, n_hid, my_e, my_h, send_slots)

    pltpu.make_async_copy(send_buf.at[my_e], recv.at[slot], recv_sem.at[my_batch]).start()

    combine_t[...] = combine.T.astype(BF)
    for i in (3, 4, 5):
        loads[i].wait()
    wi_t[...] = wi[...].T
    wo_t[...] = wo[...].T
    tok_t[...] = tok[...].T
    cot_t[...] = cot[...].T

    scale, cubic = math.sqrt(2.0 / math.pi), 0.044715
    others = pl.ds(0, n - 1)
    back_sem = len(cuts) - 1
    for b, (low, high) in enumerate(zip(cuts, cuts[1:])):
        first, rows = low, high - low
        span = pl.ds(first, rows)
        pltpu.make_async_copy(recv.at[span], recv.at[span], recv_sem.at[b]).wait()
        if b == 0:
            for c in range(CLIENTS):

                @pl.when(jnp.logical_not(jnp.logical_or(greets_first(c), me == c)))
                def _():
                    pl.semaphore_signal(
                        barrier, inc=1, device_id=(jnp.int32(0), jnp.int32(c)), device_id_type=MESH
                    )


        base = first * period
        scr_b[pl.ds(base, rows * period), :] = recv[span].astype(F32).reshape(rows * period, LANES)
        rows_in = gather_rows(scr_b, base, rows, chunks, period).astype(BF)
        rows_cot = gather_rows(scr_b, base + chunks, rows, chunks, period).astype(BF)
        pre = dot(rows_in, wi[...], 1, 0) + bi[...]
        act_grad = dot(rows_cot, wo_t[...], 1, 0)
        square = pre * pre
        tanh = jnp.tanh(scale * (pre + cubic * (square * pre)))
        cdf = 0.5 * (1.0 + tanh)
        act = (pre * cdf).astype(BF)
        slope = cdf + 0.5 * pre * (1.0 - tanh * tanh) * (scale * (1.0 + (3.0 * cubic) * square))
        pre_grad = (act_grad * slope).astype(BF)
        scatter_rows(scr_b, base, dot(act, wo[...], 1, 0), period)
        scatter_rows(scr_b, base + chunks, dot(pre_grad, wi_t[...], 1, 0), period)
        out_buf[span] = scr_b[pl.ds(base, rows * period), :].reshape((rows,) + out_buf.shape[1:]).astype(BF)

        def send_to(e, h):
            pltpu.make_async_remote_copy(
                src_ref=out_buf.at[slot_of(e * n_hid + h, n)],
                dst_ref=ret.at[me],
                send_sem=send_sem.at[1],
                recv_sem=recv_sem.at[back_sem],
                device_id=(e, h),
                device_id_type=MESH,
            ).start()

        def send_back(e, h):
            @pl.when(jnp.logical_and(e >= low, e < high))
            def _():
                pltpu.make_async_remote_copy(
                    src_ref=out_buf.at[slot_of(e * n_hid + h, n)],
                    dst_ref=ret.at[me],
                    send_sem=send_sem.at[1],
                    recv_sem=recv_sem.at[back_sem],
                    device_id=(e, h),
                    device_id_type=MESH,
                ).start()

        def send_batch(low, high):
            for dest in range(low, high):

                @pl.when(me != dest)
                def _():
                    send_to(jnp.int32(dest // n_hid), jnp.int32(dest % n_hid))

        def send_later(low, high):
            def send_back(e, h):
                place = slot_of(e * n_hid + h, n)

                @pl.when(jnp.logical_and(e >= 2, jnp.logical_and(place >= low, place < high)))
                def _():
                    send_to(e, h)

            each_peer2(n_exp, n_hid, my_e, my_h, send_back)

        if b < len(cuts) - 2:

            @pl.when(me >= CLIENTS)
            def _():
                send_batch(low, min(high, 2 * n_hid))
                if high > 2 * n_hid:
                    send_later(low, high)

        else:

            @pl.when(me < CLIENTS)
            def _():
                pl.semaphore_wait(barrier, n - 1 - FIRST)

            send_later(jnp.where(me < CLIENTS, 0, low), high)

            @pl.when(me < CLIENTS)
            def _():
                send_batch(0, 2 * n_hid)

    ret[me] = out_buf[slot]
    pltpu.make_async_copy(ret.at[others], ret.at[others], recv_sem.at[back_sem]).wait()

    total = jnp.sum(ret[...].astype(F32).reshape((n_exp, n_hid) + ret.shape[1:]), axis=1)
    scr_a[...] = total.reshape(scr_a.shape)
    slot_out[...] = gather_rows(scr_a, 0, n_exp, chunks, period).astype(BF)
    slot_grad[...] = gather_rows(scr_a, chunks, n_exp, chunks, period).astype(BF)

    def sent(count, sem):
        span = pl.ds(0, count)
        pltpu.make_async_copy(out_buf.at[span], out_buf.at[span], sem).wait()

    @pl.when(me < CLIENTS)
    def _():
        sent(sum(count for _, count, _, _ in shares) + 1, send_sem.at[0])

    @pl.when(me >= CLIENTS)
    def _():
        sent(n - 1, send_sem.at[0])

    for place, count, _, hiddens in shares:

        @pl.when(jnp.logical_and(me >= place, me < place + CLIENTS))
        def _():
            sent(count * len(hiddens) - 1, relay_sem.at[1])

    sent(n - 1, send_sem.at[1])


def finish(tok_t, cot_t, rt, dispatch_ref, combine_ref, combine_t, slot_out, slot_grad,
           mixed_hbm, grad_hbm, mixed_v, grad_v, out_sem):
    dispatch, combine = dispatch_ref[...], combine_ref[...]
    mixed_v[...] = dot(combine_t[...], slot_out[...], 1, 0).astype(BF)
    put_mixed = pltpu.make_async_copy(mixed_v, mixed_hbm.at[0], out_sem.at[0])
    put_mixed.start()
    combine_grad = dot(slot_out[...], cot_t[...], 1, 0)
    dispatch_grad = dot(slot_grad[...], tok_t[...], 1, 0)
    logit_grad = combine * (combine_grad - jnp.sum(combine * combine_grad, axis=0, keepdims=True))
    logit_grad = logit_grad + dispatch * (
        dispatch_grad - jnp.sum(dispatch * dispatch_grad, axis=1, keepdims=True)
    )
    left = jnp.concatenate([dispatch, logit_grad], axis=0).T.astype(BF)
    right = jnp.concatenate([slot_grad[...], rt[...]], axis=0)
    tokens = left.shape[0]
    half = -(-tokens // 32) * 16
    puts = [put_mixed]
    for i, (low, size) in enumerate(((0, half), (half, tokens - half))):
        span = pl.ds(low, size)
        grad_v[span, :] = dot(left[low : low + size], right, 1, 0).astype(BF)
        put = pltpu.make_async_copy(grad_v.at[span], grad_hbm.at[0, span], out_sem.at[1 + i])
        put.start()
        puts.append(put)
    for put in puts:
        put.wait()


def shards(n_exp, n_hid, tokens, router, w_in, b_in, w_out, cotangent):
    n = n_exp * n_hid
    _, m, d = tokens.shape
    f = w_in.shape[2]
    period = 2 * d // LANES
    assert tokens.shape[0] == 1 and w_in.shape[0] == 1
    any_spec = pl.BlockSpec(memory_space=pl.ANY)
    vmem_spec = pl.BlockSpec(memory_space=pltpu.VMEM)
    kept = [((d, m), BF)] * 2 + [((n_exp, d), BF)] + [((n_exp, m), F32)] * 2 + [((m, n_exp), BF)] + [((n_exp, d), BF)] * 2
    held = sum(-(-r // 8) * 8 * -(-c // LANES) * LANES * jnp.dtype(t).itemsize for (r, c), t in kept)
    grant = VMEM_BYTES - held - SLACK
    handed = pl.pallas_call(
        functools.partial(kernel, n_exp, n_hid),
        out_shape=[pltpu.VMEM(*k) for k in kept],
        in_specs=[any_spec] * 6,
        out_specs=[vmem_spec] * 8,
        scratch_shapes=[
            pltpu.VMEM((m, d), BF),
            pltpu.VMEM((m, d), BF),
            pltpu.VMEM((d, f), BF),
            pltpu.VMEM((1, f), F32),
            pltpu.VMEM((f, d), BF),
            pltpu.VMEM((f, d), BF),
            pltpu.VMEM((d, f), BF),
            pltpu.VMEM((n_exp * period, LANES), F32),
            pltpu.VMEM((n_exp, period, LANES), BF),
            pltpu.VMEM((n, period, LANES), BF),
            pltpu.VMEM((n * period, LANES), F32),
            pltpu.VMEM((n, period, LANES), BF),
            pltpu.VMEM((n, period, LANES), BF),
            pltpu.VMEM((n_exp, period, LANES), BF),
            pltpu.SemaphoreType.DMA((6,)),
            pltpu.SemaphoreType.DMA((2,)),
            pltpu.SemaphoreType.DMA((len(batch_cuts(n_exp, n_hid)),)),
            pltpu.SemaphoreType.DMA((2,)),
        ],
        compiler_params=pltpu.CompilerParams(
            collective_id=0, has_side_effects=True, vmem_limit_bytes=grant
        ),
        name="soft_moe",
    )(tokens, router.T, w_in, b_in, w_out, cotangent)
    return tuple(
        pl.pallas_call(
            finish,
            out_shape=[jax.ShapeDtypeStruct(tokens.shape, BF)] * 2,
            in_specs=[vmem_spec] * 8,
            out_specs=[any_spec] * 2,
            scratch_shapes=[
                pltpu.VMEM((m, d), BF),
                pltpu.VMEM((m, d), BF),
                pltpu.SemaphoreType.DMA((3,)),
            ],
            compiler_params=pltpu.CompilerParams(vmem_limit_bytes=48 << 20),
            name="finish",
        )(*handed)
    )


def solution(mesh):
    sizes = mesh.shape["expert"], mesh.shape["hidden"]
    return jax.shard_map(
        functools.partial(shards, *sizes),
        mesh=mesh,
        in_specs=(
            P(("expert", "hidden"), None, None),
            P(),
            P("expert", None, "hidden"),
            P("expert", "hidden"),
            P("expert", "hidden", None),
            P(("expert", "hidden"), None, None),
        ),
        out_specs=(P(("expert", "hidden"), None, None), P(("expert", "hidden"), None, None)),
        check_vma=False,
    )
```

```python
import functools
import math

import jax
import jax.numpy as jnp
from jax import lax
from jax.experimental import pallas as pl
from jax.experimental.pallas import tpu as pltpu
from jax.sharding import PartitionSpec as P

MESH = pl.DeviceIdType.MESH
BF = jnp.bfloat16
F32 = jnp.float32
LANES = 128
VMEM_BYTES = 67043328
SLACK = 4096
CLIENTS = 2
FIRST = 4


def dot(a, b, ca, cb):
    return lax.dot_general(a, b, (((ca,), (cb,)), ((), ())), preferred_element_type=F32)


def scatter_rows(scr, base, value, period):
    rows, width = value.shape
    for c in range(width // LANES):
        scr[pl.ds(base + c, rows, stride=period), :] = value[:, c * LANES : (c + 1) * LANES]


def gather_rows(scr, base, rows, chunks, period):
    parts = [scr[pl.ds(base + c, rows, stride=period), :] for c in range(chunks)]
    return jnp.concatenate(parts, axis=1)


def each_peer(n_exp, n_hid, my_e, my_h, act):
    def flip(mine, by, size):
        bit, out = 1, mine
        while bit < size:
            out = out + lax.rem(by // bit, 2) * (bit - 2 * bit * lax.rem(mine // bit, 2))
            bit *= 2
        return out

    hids = [flip(my_h, jnp.int32(j), n_hid) for j in range(n_hid)]

    def step(k, carry):
        e = flip(my_e, n_exp - k, n_exp)
        for j in reversed(range(n_hid)):
            act(e, hids[j])
        return carry

    lax.fori_loop(1, n_exp, step, 0, unroll=n_exp <= 8)
    for j in reversed(range(1, n_hid)):
        act(my_e, hids[j])


def each_peer2(n_exp, n_hid, my_e, my_h, act):
    def flip(mine, by, size):
        bit, out = 1, mine
        while bit < size:
            out = out + lax.rem(by // bit, 2) * (bit - 2 * bit * lax.rem(mine // bit, 2))
            bit *= 2
        return out

    for j in reversed(range(n_hid)):
        h = flip(my_h, jnp.int32(j), n_hid)

        def step(k, carry):
            act(flip(my_e, n_exp - k, n_exp), h)
            return carry

        lax.fori_loop(1, n_exp, step, 0, unroll=n_exp <= 8)
        if j > 0:
            act(my_e, h)


def slot_of(i, n):
    last = i >= n - n // 4
    return jnp.where(last, i - n // 2, jnp.where(i >= n // 4, i + n // 4, i))


def batch_cuts(n_exp, n_hid):
    return (0, 2, n_exp * n_hid // 2, n_exp * n_hid)


def kernel(
    n_exp, n_hid,
    tok_hbm, rt_hbm, wi_hbm, bi_hbm, wo_hbm, cot_hbm,
    tok_t, cot_t, rt, dispatch_ref, combine_ref, combine_t, slot_out, slot_grad,
    tok, cot, wi, bi, wo, wi_t, wo_t, scr_a, send_buf, recv, scr_b, out_buf, ret,
    relay, load_sem, send_sem, recv_sem, relay_sem,
):
    n = n_exp * n_hid
    my_e, my_h = lax.axis_index("expert"), lax.axis_index("hidden")
    me = my_e * n_hid + my_h
    width = tok.shape[1]
    chunks = width // LANES
    period = 2 * chunks

    loads = [
        pltpu.make_async_copy(tok_hbm.at[0], tok, load_sem.at[0]),
        pltpu.make_async_copy(rt_hbm, rt, load_sem.at[1]),
        pltpu.make_async_copy(cot_hbm.at[0], cot, load_sem.at[2]),
        pltpu.make_async_copy(wi_hbm.at[0], wi, load_sem.at[3]),
        pltpu.make_async_copy(bi_hbm, bi, load_sem.at[4]),
        pltpu.make_async_copy(wo_hbm.at[0], wo, load_sem.at[5]),
    ]
    for load in loads[:3]:
        load.start()

    cuts = batch_cuts(n_exp, n_hid)
    slot = slot_of(me, n)
    my_batch = sum((slot >= low).astype(jnp.int32) for low in cuts[1:-1])
    barrier = pltpu.get_barrier_semaphore()

    def greets_first(c):
        return functools.reduce(
            jnp.logical_or, [me == p for p in (1 - c, 2 + c, n_hid + c, 2 * n_hid + c)]
        )

    def greet(k, _):
        dest = lax.rem(me + k, n)

        @pl.when(jnp.logical_or(dest >= CLIENTS, greets_first(dest)))
        def _():
            pl.semaphore_signal(
                barrier, inc=1, device_id=(dest // n_hid, lax.rem(dest, n_hid)), device_id_type=MESH
            )

        return 0

    lax.fori_loop(1, n, greet, 0, unroll=n <= 32)
    for load in loads[3:]:
        load.start()

    loads[0].wait()
    loads[1].wait()
    rt_t = rt[...]
    logits = dot(rt_t, tok[...], 1, 1)
    up = jnp.exp(logits - jnp.max(logits, axis=1, keepdims=True))
    dispatch = up / jnp.sum(up, axis=1, keepdims=True)
    up = jnp.exp(logits - jnp.max(logits, axis=0, keepdims=True))
    combine = up / jnp.sum(up, axis=0, keepdims=True)
    dispatch_ref[...] = dispatch
    combine_ref[...] = combine
    dispatch_w = dispatch.astype(BF)
    combine_w = combine.astype(BF)

    scatter_rows(scr_a, 0, dot(dispatch_w, tok[...], 1, 0), period)
    loads[2].wait()
    scatter_rows(scr_a, chunks, dot(combine_w, cot[...], 1, 0), period)
    send_buf[...] = scr_a[...].reshape(send_buf.shape).astype(BF)


    def send_slots(e, h):
        pltpu.make_async_remote_copy(
            src_ref=send_buf.at[e],
            dst_ref=recv.at[slot],
            send_sem=send_sem.at[0],
            recv_sem=recv_sem.at[my_batch],
            device_id=(e, h),
            device_id_type=MESH,
        ).start()

    def lend(e, dest):
        pltpu.make_async_remote_copy(
            src_ref=send_buf.at[e],
            dst_ref=relay.at[e],
            send_sem=send_sem.at[0],
            recv_sem=relay_sem.at[0],
            device_id=dest,
            device_id_type=MESH,
        ).start()

    def each(count, act):
        lax.fori_loop(0, count, lambda k, _: (act(k), 0)[1], 0, unroll=count <= 8)

    half = n_exp // 2
    shares = (
        (2, half + 1, lambda k: jnp.maximum(n_exp - 1 - 2 * k, 0), range(2, n_hid)),
        (n_hid, half, lambda k: n_exp - 1 - 2 * k, range(2)),
        (2 * n_hid, half - 1, lambda k: n_exp - 2 - 2 * k, range(n_hid)),
    )

    @pl.when(me < CLIENTS)
    def _():
        pl.semaphore_wait(barrier, FIRST)
        for place, count, expert, _ in shares:
            dest = (jnp.int32(place // n_hid), place % n_hid + my_h)
            each(count, lambda k: lend(expert(k), dest))
        send_slots(jnp.int32(0), 1 - my_h)

    @pl.when(me >= CLIENTS)
    def _():
        pl.semaphore_wait(barrier, n - 1)

    for place, count, expert, hiddens in shares:
        client = me - place

        @pl.when(jnp.logical_and(client >= 0, client < CLIENTS))
        def _():
            lent = pl.ds(0, count)
            pltpu.make_async_copy(relay.at[lent], relay.at[lent], relay_sem.at[0]).wait()

            def hand(k):
                for h in reversed(hiddens):

                    @pl.when(expert(k) * n_hid + h != me)
                    def _():
                        pltpu.make_async_remote_copy(
                            src_ref=relay.at[expert(k)],
                            dst_ref=recv.at[client],
                            send_sem=relay_sem.at[1],
                            recv_sem=recv_sem.at[0],
                            device_id=(jnp.int32(0) + expert(k), jnp.int32(h)),
                            device_id_type=MESH,
                        ).start()

            each(count, hand)
            pltpu.make_async_copy(relay.at[my_e], recv.at[client], recv_sem.at[0]).start()

    @pl.when(me >= CLIENTS)
    def _():
        each_peer(n_exp, n_hid, my_e, my_h, send_slots)

    pltpu.make_async_copy(send_buf.at[my_e], recv.at[slot], recv_sem.at[my_batch]).start()

    combine_t[...] = combine.T.astype(BF)
    for i in (3, 4, 5):
        loads[i].wait()
    wi_t[...] = wi[...].T
    wo_t[...] = wo[...].T
    tok_t[...] = tok[...].T
    cot_t[...] = cot[...].T

    scale, cubic = math.sqrt(2.0 / math.pi), 0.044715
    others = pl.ds(0, n - 1)
    back_sem = len(cuts) - 1
    for b, (low, high) in enumerate(zip(cuts, cuts[1:])):
        first, rows = low, high - low
        span = pl.ds(first, rows)
        pltpu.make_async_copy(recv.at[span], recv.at[span], recv_sem.at[b]).wait()
        if b == 0:
            for c in range(CLIENTS):

                @pl.when(jnp.logical_not(jnp.logical_or(greets_first(c), me == c)))
                def _():
                    pl.semaphore_signal(
                        barrier, inc=1, device_id=(jnp.int32(0), jnp.int32(c)), device_id_type=MESH
                    )


        base = first * period
        scr_b[pl.ds(base, rows * period), :] = recv[span].astype(F32).reshape(rows * period, LANES)
        rows_in = gather_rows(scr_b, base, rows, chunks, period).astype(BF)
        rows_cot = gather_rows(scr_b, base + chunks, rows, chunks, period).astype(BF)
        pre = dot(rows_in, wi[...], 1, 0) + bi[...]
        act_grad = dot(rows_cot, wo_t[...], 1, 0)
        square = pre * pre
        tanh = jnp.tanh(scale * (pre + cubic * (square * pre)))
        cdf = 0.5 * (1.0 + tanh)
        act = (pre * cdf).astype(BF)
        slope = cdf + 0.5 * pre * (1.0 - tanh * tanh) * (scale * (1.0 + (3.0 * cubic) * square))
        pre_grad = (act_grad * slope).astype(BF)
        scatter_rows(scr_b, base, dot(act, wo[...], 1, 0), period)
        scatter_rows(scr_b, base + chunks, dot(pre_grad, wi_t[...], 1, 0), period)
        out_buf[span] = scr_b[pl.ds(base, rows * period), :].reshape((rows,) + out_buf.shape[1:]).astype(BF)

        def send_to(e, h):
            pltpu.make_async_remote_copy(
                src_ref=out_buf.at[slot_of(e * n_hid + h, n)],
                dst_ref=ret.at[me],
                send_sem=send_sem.at[1],
                recv_sem=recv_sem.at[back_sem],
                device_id=(e, h),
                device_id_type=MESH,
            ).start()

        def send_back(e, h):
            @pl.when(jnp.logical_and(e >= low, e < high))
            def _():
                pltpu.make_async_remote_copy(
                    src_ref=out_buf.at[slot_of(e * n_hid + h, n)],
                    dst_ref=ret.at[me],
                    send_sem=send_sem.at[1],
                    recv_sem=recv_sem.at[back_sem],
                    device_id=(e, h),
                    device_id_type=MESH,
                ).start()

        def send_batch(low, high):
            for dest in range(low, high):

                @pl.when(me != dest)
                def _():
                    send_to(jnp.int32(dest // n_hid), jnp.int32(dest % n_hid))

        def send_later(low, high):
            def send_back(e, h):
                place = slot_of(e * n_hid + h, n)

                @pl.when(jnp.logical_and(e >= 2, jnp.logical_and(place >= low, place < high)))
                def _():
                    send_to(e, h)

            each_peer2(n_exp, n_hid, my_e, my_h, send_back)

        if b < len(cuts) - 2:

            @pl.when(me >= CLIENTS)
            def _():
                send_batch(low, min(high, 2 * n_hid))
                if high > 2 * n_hid:
                    send_later(low, high)

        else:

            @pl.when(me < CLIENTS)
            def _():
                pl.semaphore_wait(barrier, n - 1 - FIRST)

            send_later(jnp.where(me < CLIENTS, 0, low), high)

            @pl.when(me < CLIENTS)
            def _():
                send_batch(0, 2 * n_hid)

    ret[me] = out_buf[slot]
    pltpu.make_async_copy(ret.at[others], ret.at[others], recv_sem.at[back_sem]).wait()

    total = jnp.sum(ret[...].astype(F32).reshape((n_exp, n_hid) + ret.shape[1:]), axis=1)
    scr_a[...] = total.reshape(scr_a.shape)
    slot_out[...] = gather_rows(scr_a, 0, n_exp, chunks, period).astype(BF)
    slot_grad[...] = gather_rows(scr_a, chunks, n_exp, chunks, period).astype(BF)

    def sent(count, sem):
        span = pl.ds(0, count)
        pltpu.make_async_copy(out_buf.at[span], out_buf.at[span], sem).wait()

    @pl.when(me < CLIENTS)
    def _():
        sent(sum(count for _, count, _, _ in shares) + 1, send_sem.at[0])

    @pl.when(me >= CLIENTS)
    def _():
        sent(n - 1, send_sem.at[0])

    for place, count, _, hiddens in shares:

        @pl.when(jnp.logical_and(me >= place, me < place + CLIENTS))
        def _():
            sent(count * len(hiddens) - 1, relay_sem.at[1])

    sent(n - 1, send_sem.at[1])


def finish(tok_t, cot_t, rt, dispatch_ref, combine_ref, combine_t, slot_out, slot_grad,
           mixed_hbm, grad_hbm, mixed_v, grad_v, out_sem):
    dispatch, combine = dispatch_ref[...], combine_ref[...]
    combine_grad = dot(slot_out[...], cot_t[...], 1, 0)
    dispatch_grad = dot(slot_grad[...], tok_t[...], 1, 0)
    mixed_v[...] = dot(combine_t[...], slot_out[...], 1, 0).astype(BF)
    logit_grad = combine * (combine_grad - jnp.sum(combine * combine_grad, axis=0, keepdims=True))
    logit_grad = logit_grad + dispatch * (
        dispatch_grad - jnp.sum(dispatch * dispatch_grad, axis=1, keepdims=True)
    )
    left = jnp.concatenate([dispatch, logit_grad], axis=0).T.astype(BF)
    right = jnp.concatenate([slot_grad[...], rt[...]], axis=0)
    grad_v[...] = dot(left, right, 1, 0).astype(BF)
    puts = [
        pltpu.make_async_copy(mixed_v, mixed_hbm.at[0], out_sem.at[0]),
        pltpu.make_async_copy(grad_v, grad_hbm.at[0], out_sem.at[1]),
    ]
    for put in puts:
        put.start()
    for put in puts:
        put.wait()


def shards(n_exp, n_hid, tokens, router, w_in, b_in, w_out, cotangent):
    n = n_exp * n_hid
    _, m, d = tokens.shape
    f = w_in.shape[2]
    period = 2 * d // LANES
    assert tokens.shape[0] == 1 and w_in.shape[0] == 1
    any_spec = pl.BlockSpec(memory_space=pl.ANY)
    vmem_spec = pl.BlockSpec(memory_space=pltpu.VMEM)
    kept = [((d, m), BF)] * 2 + [((n_exp, d), BF)] + [((n_exp, m), F32)] * 2 + [((m, n_exp), BF)] + [((n_exp, d), BF)] * 2
    held = sum(-(-r // 8) * 8 * -(-c // LANES) * LANES * jnp.dtype(t).itemsize for (r, c), t in kept)
    grant = VMEM_BYTES - held - SLACK
    handed = pl.pallas_call(
        functools.partial(kernel, n_exp, n_hid),
        out_shape=[pltpu.VMEM(*k) for k in kept],
        in_specs=[any_spec] * 6,
        out_specs=[vmem_spec] * 8,
        scratch_shapes=[
            pltpu.VMEM((m, d), BF),
            pltpu.VMEM((m, d), BF),
            pltpu.VMEM((d, f), BF),
            pltpu.VMEM((1, f), F32),
            pltpu.VMEM((f, d), BF),
            pltpu.VMEM((f, d), BF),
            pltpu.VMEM((d, f), BF),
            pltpu.VMEM((n_exp * period, LANES), F32),
            pltpu.VMEM((n_exp, period, LANES), BF),
            pltpu.VMEM((n, period, LANES), BF),
            pltpu.VMEM((n * period, LANES), F32),
            pltpu.VMEM((n, period, LANES), BF),
            pltpu.VMEM((n, period, LANES), BF),
            pltpu.VMEM((n_exp, period, LANES), BF),
            pltpu.SemaphoreType.DMA((6,)),
            pltpu.SemaphoreType.DMA((2,)),
            pltpu.SemaphoreType.DMA((len(batch_cuts(n_exp, n_hid)),)),
            pltpu.SemaphoreType.DMA((2,)),
        ],
        compiler_params=pltpu.CompilerParams(
            collective_id=0, has_side_effects=True, vmem_limit_bytes=grant
        ),
        name="soft_moe",
    )(tokens, router.T, w_in, b_in, w_out, cotangent)
    return tuple(
        pl.pallas_call(
            finish,
            out_shape=[jax.ShapeDtypeStruct(tokens.shape, BF)] * 2,
            in_specs=[vmem_spec] * 8,
            out_specs=[any_spec] * 2,
            scratch_shapes=[
                pltpu.VMEM((m, d), BF),
                pltpu.VMEM((m, d), BF),
                pltpu.SemaphoreType.DMA((2,)),
            ],
            compiler_params=pltpu.CompilerParams(vmem_limit_bytes=48 << 20),
            name="finish",
        )(*handed)
    )


def solution(mesh):
    sizes = mesh.shape["expert"], mesh.shape["hidden"]
    return jax.shard_map(
        functools.partial(shards, *sizes),
        mesh=mesh,
        in_specs=(
            P(("expert", "hidden"), None, None),
            P(),
            P("expert", None, "hidden"),
            P("expert", "hidden"),
            P("expert", "hidden", None),
            P(("expert", "hidden"), None, None),
        ),
        out_specs=(P(("expert", "hidden"), None, None), P(("expert", "hidden"), None, None)),
        check_vma=False,
    )
```

```python
import functools
import math

import jax
import jax.numpy as jnp
from jax import lax
from jax.experimental import pallas as pl
from jax.experimental.pallas import tpu as pltpu
from jax.sharding import PartitionSpec as P

MESH = pl.DeviceIdType.MESH
BF = jnp.bfloat16
F32 = jnp.float32
LANES = 128
VMEM_BYTES = 67043328
SLACK = 4096
CLIENTS = 2
FIRST = 4


def dot(a, b, ca, cb):
    return lax.dot_general(a, b, (((ca,), (cb,)), ((), ())), preferred_element_type=F32)


def scatter_rows(scr, base, value, period):
    rows, width = value.shape
    for c in range(width // LANES):
        scr[pl.ds(base + c, rows, stride=period), :] = value[:, c * LANES : (c + 1) * LANES]


def gather_rows(scr, base, rows, chunks, period):
    parts = [scr[pl.ds(base + c, rows, stride=period), :] for c in range(chunks)]
    return jnp.concatenate(parts, axis=1)


def each_peer(n_exp, n_hid, my_e, my_h, act):
    def flip(mine, by, size):
        bit, out = 1, mine
        while bit < size:
            out = out + lax.rem(by // bit, 2) * (bit - 2 * bit * lax.rem(mine // bit, 2))
            bit *= 2
        return out

    hids = [flip(my_h, jnp.int32(j), n_hid) for j in range(n_hid)]

    def step(k, carry):
        e = flip(my_e, n_exp - k, n_exp)
        for j in reversed(range(n_hid)):
            act(e, hids[j])
        return carry

    lax.fori_loop(1, n_exp, step, 0, unroll=n_exp <= 8)
    for j in reversed(range(1, n_hid)):
        act(my_e, hids[j])


def each_peer2(n_exp, n_hid, my_e, my_h, act):
    def flip(mine, by, size):
        bit, out = 1, mine
        while bit < size:
            out = out + lax.rem(by // bit, 2) * (bit - 2 * bit * lax.rem(mine // bit, 2))
            bit *= 2
        return out

    for j in reversed(range(n_hid)):
        h = flip(my_h, jnp.int32(j), n_hid)

        def step(k, carry):
            act(flip(my_e, n_exp - k, n_exp), h)
            return carry

        lax.fori_loop(1, n_exp, step, 0, unroll=n_exp <= 8)
        if j > 0:
            act(my_e, h)


def slot_of(i, n):
    last = i >= n - n // 4
    return jnp.where(last, i - n // 2, jnp.where(i >= n // 4, i + n // 4, i))


def batch_cuts(n_exp, n_hid):
    return (0, 2, n_exp * n_hid // 2, n_exp * n_hid)


def kernel(
    n_exp, n_hid,
    tok_hbm, rt_hbm, wi_hbm, bi_hbm, wo_hbm, cot_hbm,
    tok_t, cot_t, rt, dispatch_ref, combine_ref, combine_t, slot_out, slot_grad,
    tok, cot, wi, bi, wo, wi_t, wo_t, scr_a, send_buf, recv, scr_b, out_buf, ret,
    relay, load_sem, send_sem, recv_sem, relay_sem,
):
    n = n_exp * n_hid
    my_e, my_h = lax.axis_index("expert"), lax.axis_index("hidden")
    me = my_e * n_hid + my_h
    width = tok.shape[1]
    chunks = width // LANES
    period = 2 * chunks

    loads = [
        pltpu.make_async_copy(tok_hbm.at[0], tok, load_sem.at[0]),
        pltpu.make_async_copy(rt_hbm, rt, load_sem.at[1]),
        pltpu.make_async_copy(cot_hbm.at[0], cot, load_sem.at[2]),
        pltpu.make_async_copy(wi_hbm.at[0], wi, load_sem.at[3]),
        pltpu.make_async_copy(bi_hbm, bi, load_sem.at[4]),
        pltpu.make_async_copy(wo_hbm.at[0], wo, load_sem.at[5]),
    ]
    for load in loads[:3]:
        load.start()

    cuts = batch_cuts(n_exp, n_hid)
    slot = slot_of(me, n)
    my_batch = sum((slot >= low).astype(jnp.int32) for low in cuts[1:-1])
    barrier = pltpu.get_barrier_semaphore()

    def greets_first(c):
        return functools.reduce(
            jnp.logical_or, [me == p for p in (1 - c, 2 + c, n_hid + c, 2 * n_hid + c)]
        )

    def greet(k, _):
        dest = lax.rem(me + k, n)

        @pl.when(jnp.logical_or(dest >= CLIENTS, greets_first(dest)))
        def _():
            pl.semaphore_signal(
                barrier, inc=1, device_id=(dest // n_hid, lax.rem(dest, n_hid)), device_id_type=MESH
            )

        return 0

    lax.fori_loop(1, n, greet, 0, unroll=n <= 32)
    for load in loads[3:]:
        load.start()

    loads[0].wait()
    loads[1].wait()
    rt_t = rt[...]
    logits = dot(rt_t, tok[...], 1, 1)
    up = jnp.exp(logits - jnp.max(logits, axis=1, keepdims=True))
    dispatch = up / jnp.sum(up, axis=1, keepdims=True)
    up = jnp.exp(logits - jnp.max(logits, axis=0, keepdims=True))
    combine = up / jnp.sum(up, axis=0, keepdims=True)
    dispatch_ref[...] = dispatch
    combine_ref[...] = combine
    dispatch_w = dispatch.astype(BF)
    combine_w = combine.astype(BF)

    scatter_rows(scr_a, 0, dot(dispatch_w, tok[...], 1, 0), period)
    loads[2].wait()
    scatter_rows(scr_a, chunks, dot(combine_w, cot[...], 1, 0), period)
    send_buf[...] = scr_a[...].reshape(send_buf.shape).astype(BF)


    def send_slots(e, h):
        pltpu.make_async_remote_copy(
            src_ref=send_buf.at[e],
            dst_ref=recv.at[slot],
            send_sem=send_sem.at[0],
            recv_sem=recv_sem.at[my_batch],
            device_id=(e, h),
            device_id_type=MESH,
        ).start()

    def lend(e, dest):
        pltpu.make_async_remote_copy(
            src_ref=send_buf.at[e],
            dst_ref=relay.at[e],
            send_sem=send_sem.at[0],
            recv_sem=relay_sem.at[0],
            device_id=dest,
            device_id_type=MESH,
        ).start()

    def each(count, act):
        lax.fori_loop(0, count, lambda k, _: (act(k), 0)[1], 0, unroll=count <= 8)

    half = n_exp // 2
    shares = (
        (2 * n_hid, half - 1, lambda k: n_exp - 2 - 2 * k, range(n_hid)),
        (2, half + 1, lambda k: jnp.maximum(n_exp - 1 - 2 * k, 0), range(2, n_hid)),
        (n_hid, half, lambda k: n_exp - 1 - 2 * k, range(2)),
    )

    @pl.when(me < CLIENTS)
    def _():
        pl.semaphore_wait(barrier, FIRST)
        for place, count, expert, _ in shares:
            dest = (jnp.int32(place // n_hid), place % n_hid + my_h)
            each(count, lambda k: lend(expert(k), dest))
        send_slots(jnp.int32(0), 1 - my_h)

    @pl.when(me >= CLIENTS)
    def _():
        pl.semaphore_wait(barrier, n - 1)

    for place, count, expert, hiddens in shares:
        client = me - place

        @pl.when(jnp.logical_and(client >= 0, client < CLIENTS))
        def _():
            lent = pl.ds(0, count)
            pltpu.make_async_copy(relay.at[lent], relay.at[lent], relay_sem.at[0]).wait()

            def hand(k):
                for h in reversed(hiddens):

                    @pl.when(expert(k) * n_hid + h != me)
                    def _():
                        pltpu.make_async_remote_copy(
                            src_ref=relay.at[expert(k)],
                            dst_ref=recv.at[client],
                            send_sem=relay_sem.at[1],
                            recv_sem=recv_sem.at[0],
                            device_id=(jnp.int32(0) + expert(k), jnp.int32(h)),
                            device_id_type=MESH,
                        ).start()

            each(count, hand)
            pltpu.make_async_copy(relay.at[my_e], recv.at[client], recv_sem.at[0]).start()

    @pl.when(me >= CLIENTS)
    def _():
        each_peer(n_exp, n_hid, my_e, my_h, send_slots)

    pltpu.make_async_copy(send_buf.at[my_e], recv.at[slot], recv_sem.at[my_batch]).start()

    combine_t[...] = combine.T.astype(BF)
    for i in (3, 4, 5):
        loads[i].wait()
    wi_t[...] = wi[...].T
    wo_t[...] = wo[...].T
    tok_t[...] = tok[...].T
    cot_t[...] = cot[...].T

    scale, cubic = math.sqrt(2.0 / math.pi), 0.044715
    others = pl.ds(0, n - 1)
    back_sem = len(cuts) - 1
    for b, (low, high) in enumerate(zip(cuts, cuts[1:])):
        first, rows = low, high - low
        span = pl.ds(first, rows)
        pltpu.make_async_copy(recv.at[span], recv.at[span], recv_sem.at[b]).wait()
        if b == 0:
            for c in range(CLIENTS):

                @pl.when(jnp.logical_not(jnp.logical_or(greets_first(c), me == c)))
                def _():
                    pl.semaphore_signal(
                        barrier, inc=1, device_id=(jnp.int32(0), jnp.int32(c)), device_id_type=MESH
                    )


        base = first * period
        scr_b[pl.ds(base, rows * period), :] = recv[span].astype(F32).reshape(rows * period, LANES)
        rows_in = gather_rows(scr_b, base, rows, chunks, period).astype(BF)
        rows_cot = gather_rows(scr_b, base + chunks, rows, chunks, period).astype(BF)
        pre = dot(rows_in, wi[...], 1, 0) + bi[...]
        act_grad = dot(rows_cot, wo_t[...], 1, 0)
        square = pre * pre
        tanh = jnp.tanh(scale * (pre + cubic * (square * pre)))
        cdf = 0.5 * (1.0 + tanh)
        act = (pre * cdf).astype(BF)
        slope = cdf + 0.5 * pre * (1.0 - tanh * tanh) * (scale * (1.0 + (3.0 * cubic) * square))
        pre_grad = (act_grad * slope).astype(BF)
        scatter_rows(scr_b, base, dot(act, wo[...], 1, 0), period)
        scatter_rows(scr_b, base + chunks, dot(pre_grad, wi_t[...], 1, 0), period)
        out_buf[span] = scr_b[pl.ds(base, rows * period), :].reshape((rows,) + out_buf.shape[1:]).astype(BF)

        def send_to(e, h):
            pltpu.make_async_remote_copy(
                src_ref=out_buf.at[slot_of(e * n_hid + h, n)],
                dst_ref=ret.at[me],
                send_sem=send_sem.at[1],
                recv_sem=recv_sem.at[back_sem],
                device_id=(e, h),
                device_id_type=MESH,
            ).start()

        def send_back(e, h):
            @pl.when(jnp.logical_and(e >= low, e < high))
            def _():
                pltpu.make_async_remote_copy(
                    src_ref=out_buf.at[slot_of(e * n_hid + h, n)],
                    dst_ref=ret.at[me],
                    send_sem=send_sem.at[1],
                    recv_sem=recv_sem.at[back_sem],
                    device_id=(e, h),
                    device_id_type=MESH,
                ).start()

        def send_batch(low, high):
            for dest in range(low, high):

                @pl.when(me != dest)
                def _():
                    send_to(jnp.int32(dest // n_hid), jnp.int32(dest % n_hid))

        def send_later(low, high):
            def send_back(e, h):
                place = slot_of(e * n_hid + h, n)

                @pl.when(jnp.logical_and(e >= 2, jnp.logical_and(place >= low, place < high)))
                def _():
                    send_to(e, h)

            each_peer2(n_exp, n_hid, my_e, my_h, send_back)

        if b < len(cuts) - 2:

            @pl.when(me >= CLIENTS)
            def _():
                send_batch(low, min(high, 2 * n_hid))
                if high > 2 * n_hid:
                    send_later(low, high)

        else:

            @pl.when(me < CLIENTS)
            def _():
                pl.semaphore_wait(barrier, n - 1 - FIRST)

            send_later(jnp.where(me < CLIENTS, 0, low), high)

            @pl.when(me < CLIENTS)
            def _():
                send_batch(0, 2 * n_hid)

    ret[me] = out_buf[slot]
    pltpu.make_async_copy(ret.at[others], ret.at[others], recv_sem.at[back_sem]).wait()

    total = jnp.sum(ret[...].astype(F32).reshape((n_exp, n_hid) + ret.shape[1:]), axis=1)
    scr_a[...] = total.reshape(scr_a.shape)
    slot_out[...] = gather_rows(scr_a, 0, n_exp, chunks, period).astype(BF)
    slot_grad[...] = gather_rows(scr_a, chunks, n_exp, chunks, period).astype(BF)

    def sent(count, sem):
        span = pl.ds(0, count)
        pltpu.make_async_copy(out_buf.at[span], out_buf.at[span], sem).wait()

    @pl.when(me < CLIENTS)
    def _():
        sent(sum(count for _, count, _, _ in shares) + 1, send_sem.at[0])

    @pl.when(me >= CLIENTS)
    def _():
        sent(n - 1, send_sem.at[0])

    for place, count, _, hiddens in shares:

        @pl.when(jnp.logical_and(me >= place, me < place + CLIENTS))
        def _():
            sent(count * len(hiddens) - 1, relay_sem.at[1])

    sent(n - 1, send_sem.at[1])


def finish(tok_t, cot_t, rt, dispatch_ref, combine_ref, combine_t, slot_out, slot_grad,
           mixed_hbm, grad_hbm, mixed_v, grad_v, out_sem):
    dispatch, combine = dispatch_ref[...], combine_ref[...]
    combine_grad = dot(slot_out[...], cot_t[...], 1, 0)
    dispatch_grad = dot(slot_grad[...], tok_t[...], 1, 0)
    mixed_v[...] = dot(combine_t[...], slot_out[...], 1, 0).astype(BF)
    logit_grad = combine * (combine_grad - jnp.sum(combine * combine_grad, axis=0, keepdims=True))
    logit_grad = logit_grad + dispatch * (
        dispatch_grad - jnp.sum(dispatch * dispatch_grad, axis=1, keepdims=True)
    )
    left = jnp.concatenate([dispatch, logit_grad], axis=0).T.astype(BF)
    right = jnp.concatenate([slot_grad[...], rt[...]], axis=0)
    grad_v[...] = dot(left, right, 1, 0).astype(BF)
    puts = [
        pltpu.make_async_copy(mixed_v, mixed_hbm.at[0], out_sem.at[0]),
        pltpu.make_async_copy(grad_v, grad_hbm.at[0], out_sem.at[1]),
    ]
    for put in puts:
        put.start()
    for put in puts:
        put.wait()


def shards(n_exp, n_hid, tokens, router, w_in, b_in, w_out, cotangent):
    n = n_exp * n_hid
    _, m, d = tokens.shape
    f = w_in.shape[2]
    period = 2 * d // LANES
    assert tokens.shape[0] == 1 and w_in.shape[0] == 1
    any_spec = pl.BlockSpec(memory_space=pl.ANY)
    vmem_spec = pl.BlockSpec(memory_space=pltpu.VMEM)
    kept = [((d, m), BF)] * 2 + [((n_exp, d), BF)] + [((n_exp, m), F32)] * 2 + [((m, n_exp), BF)] + [((n_exp, d), BF)] * 2
    held = sum(-(-r // 8) * 8 * -(-c // LANES) * LANES * jnp.dtype(t).itemsize for (r, c), t in kept)
    grant = VMEM_BYTES - held - SLACK
    handed = pl.pallas_call(
        functools.partial(kernel, n_exp, n_hid),
        out_shape=[pltpu.VMEM(*k) for k in kept],
        in_specs=[any_spec] * 6,
        out_specs=[vmem_spec] * 8,
        scratch_shapes=[
            pltpu.VMEM((m, d), BF),
            pltpu.VMEM((m, d), BF),
            pltpu.VMEM((d, f), BF),
            pltpu.VMEM((1, f), F32),
            pltpu.VMEM((f, d), BF),
            pltpu.VMEM((f, d), BF),
            pltpu.VMEM((d, f), BF),
            pltpu.VMEM((n_exp * period, LANES), F32),
            pltpu.VMEM((n_exp, period, LANES), BF),
            pltpu.VMEM((n, period, LANES), BF),
            pltpu.VMEM((n * period, LANES), F32),
            pltpu.VMEM((n, period, LANES), BF),
            pltpu.VMEM((n, period, LANES), BF),
            pltpu.VMEM((n_exp, period, LANES), BF),
            pltpu.SemaphoreType.DMA((6,)),
            pltpu.SemaphoreType.DMA((2,)),
            pltpu.SemaphoreType.DMA((len(batch_cuts(n_exp, n_hid)),)),
            pltpu.SemaphoreType.DMA((2,)),
        ],
        compiler_params=pltpu.CompilerParams(
            collective_id=0, has_side_effects=True, vmem_limit_bytes=grant
        ),
        name="soft_moe",
    )(tokens, router.T, w_in, b_in, w_out, cotangent)
    return tuple(
        pl.pallas_call(
            finish,
            out_shape=[jax.ShapeDtypeStruct(tokens.shape, BF)] * 2,
            in_specs=[vmem_spec] * 8,
            out_specs=[any_spec] * 2,
            scratch_shapes=[
                pltpu.VMEM((m, d), BF),
                pltpu.VMEM((m, d), BF),
                pltpu.SemaphoreType.DMA((2,)),
            ],
            compiler_params=pltpu.CompilerParams(vmem_limit_bytes=48 << 20),
            name="finish",
        )(*handed)
    )


def solution(mesh):
    sizes = mesh.shape["expert"], mesh.shape["hidden"]
    return jax.shard_map(
        functools.partial(shards, *sizes),
        mesh=mesh,
        in_specs=(
            P(("expert", "hidden"), None, None),
            P(),
            P("expert", None, "hidden"),
            P("expert", "hidden"),
            P("expert", "hidden", None),
            P(("expert", "hidden"), None, None),
        ),
        out_specs=(P(("expert", "hidden"), None, None), P(("expert", "hidden"), None, None)),
        check_vma=False,
    )
```
